512 devices in a mesh: af: 16 (over z, core), gy: 4 (over x), gz: 8 (over y).
Axes of the slice: x: 4, y: 8, z: 8, core: 2. Of those that a mesh axis runs over, the one named last changes fastest.
Arguments:
- slab: bfloat16 [512, 262144], P('af', ('gy', 'gz')), may hold values from -4000 to 4000
- block_owner: int32 [4, 8, 16], P('gy', 'gz'), may hold values from 0 to 15, each once within a row
- basis_init: float32 [512, 128], replicated, may hold values from -0.25 to 0.25
Outputs:
- triangle: float32 [512, 512], replicated
- basis: float32 [512, 128], replicated
- core: bfloat16 [128, 262144], P(None, ('gy', 'gz', 'af'))
The draws below stay inside these ranges and needn't reach their ends.
Inputs may be any that keep to these rules, and one draw needn't show every extreme that they name: For every gy and gz index, block_owner[gy, gz, :] is a permutation of the 16 af indices.
All inputs are finite; a program needn't handle non-finite values.
Results may differ from the reference program's by a relative error of at most 0.0049.
Values may be sent and summed in bfloat16 or wider, within the bound.
A program may use at most 64 MiB of HBM per device.

```python
import math
import jax
import jax.numpy as jnp
from jax import lax

ROWS = 512
RANK = 128
CDEV = 512
ITERS = 2
AF_DEVS = 16
GY_DEVS = 4
GZ_DEVS = 8
COLS = 262144


def draw_slab(key, part):
    base = jax.random.fold_in(key, 11)
    key_mix, key_rows, key_noise, key_cols, key_coef = jax.random.split(base, 5)
    decay = jnp.exp(-math.log(2.0) * jnp.arange(ROWS, dtype=jnp.float32) / ROWS)
    mixing = (jnp.eye(ROWS, dtype=jnp.float32) + 0.3 * jax.random.normal(key_mix, (ROWS, ROWS), jnp.float32) / math.sqrt(ROWS)) * decay[None, :]
    position = jnp.arange(COLS, dtype=jnp.float32) / COLS
    row_scale = jnp.exp(jax.random.uniform(key_rows, (ROWS, 1), jnp.float32, 0.0, math.log(10.0)))
    coef = jax.random.truncated_normal(key_coef, -4.0, 4.0, (ROWS, COLS), jnp.float32)
    noise = 0.05 * jax.random.truncated_normal(key_noise, -4.0, 4.0, (ROWS, COLS), jnp.float32)
    rising = jnp.exp(math.log(3.0) * position)
    col_scale = jnp.exp(jax.random.uniform(key_cols, (COLS,), jnp.float32, 0.0, math.log(3.5))) * rising
    mixed = jnp.dot(mixing, coef, precision=lax.Precision.HIGHEST)
    values = row_scale * (mixed + noise) * col_scale[None, :]
    return values.astype(jnp.bfloat16)


def centred(key, shape, width, most, held_as=jnp.bfloat16):
    entries = width * jax.random.normal(key, shape, jnp.float32)
    return jnp.clip(entries, min=-most, max=most).astype(held_as)


def setup_inputs(seed: int = 0) -> dict:
    arg_keys = jax.random.split(jax.random.key(seed), 4)
    slab = draw_slab(jax.random.fold_in(arg_keys[3], 71), 0)
    block_owner = jax.vmap(lambda own: jax.random.permutation(own, AF_DEVS))(jax.random.split(arg_keys[1], GY_DEVS * GZ_DEVS)).reshape((GY_DEVS, GZ_DEVS, AF_DEVS)).astype(jnp.int32)
    basis_init = centred(arg_keys[2], (ROWS, RANK), ROWS ** -0.5, 0.25, jnp.float32)
    return dict(slab=slab, block_owner=block_owner, basis_init=basis_init)


exact_mode = lax.Precision.HIGHEST

def orthonormal(matrix):
    inner_prod = jnp.dot(matrix.T, matrix, precision=exact_mode)
    factor = jnp.linalg.cholesky(inner_prod)
    return lax.linalg.triangular_solve(factor, matrix, left_side=False, lower=True, transpose_a=True)

def reference(slab, block_owner, basis_init):
    gram = jnp.dot(slab.astype(jnp.float32), slab.T.astype(jnp.float32), preferred_element_type=jnp.float32) / COLS
    triangle = jnp.linalg.cholesky(gram)
    basis = basis_init
    for sweep in range(ITERS):
        half_basis = orthonormal(jnp.dot(triangle.T, basis, precision=exact_mode))
        basis = orthonormal(jnp.dot(triangle, half_basis, precision=exact_mode))
    narrow = basis.astype(jnp.bfloat16)
    projected = jnp.dot(narrow.T.astype(jnp.float32), slab.astype(jnp.float32), preferred_element_type=jnp.float32).astype(jnp.bfloat16)
    groups = GY_DEVS * GZ_DEVS
    blocks = projected.reshape(RANK, groups, AF_DEVS, CDEV)
    owners = block_owner.reshape(groups, AF_DEVS).astype(jnp.int32)
    source = jnp.argsort(owners, axis=1).astype(jnp.int32)
    index_full = jnp.broadcast_to(source[None, :, :, None], blocks.shape)
    core = jnp.take_along_axis(blocks, index_full, axis=2).reshape(RANK, COLS)
    return (triangle, basis, core)
```

```python
import functools
import jax
import jax.numpy as jnp
from jax import lax
from jax.experimental import pallas as pl
from jax.experimental.pallas import tpu as pltpu
from jax.sharding import PartitionSpec as P

ITERS = 2
TILE = 128
MESH = pl.DeviceIdType.MESH


def ring_offsets(size):
    return sorted(range(1, size), key=lambda step: -min(step, size - step))


def exchange_kernel(
    sizes, outgoing, columns_ref, gram_ref,
    part, pair_land, pair_sum, x_land, x_sum, y_land, z_land, y_gather, x_gather,
    a2a_send, a2a_recv, pair_send, pair_recv, x_send, x_recv, y_send, y_recv, z_send, z_recv,
    yg_send, yg_recv, xg_send, xg_recv, final_send, final_recv,
):
    fibers, x_size, y_size = sizes
    z_size = fibers // 2
    rows, block_cols = outgoing.shape[1:]
    fiber = lax.axis_index("af")
    x = lax.axis_index("gy")
    y = lax.axis_index("gz")
    z, core = fiber // 2, fiber % 2
    half = pair_sum.shape[0]
    x_rows = x_sum.shape[0]
    y_rows = y_land.shape[1]

    def fiber_at(z_step, core_step):
        return ((z + z_step) % z_size) * 2 + (core + core_step) % 2

    fiber_steps = [(s, c) for s in ring_offsets(z_size) for c in (0, 1)] + [(0, 1)]
    barrier = pltpu.get_barrier_semaphore()
    for z_step, core_step in fiber_steps:
        pl.semaphore_signal(barrier, inc=1, device_id={"af": fiber_at(z_step, core_step)}, device_id_type=MESH)
    for step in range(1, y_size):
        pl.semaphore_signal(barrier, inc=1, device_id={"gz": (y + step) % y_size}, device_id_type=MESH)
    for step in range(1, x_size):
        pl.semaphore_signal(barrier, inc=1, device_id={"gy": (x + step) % x_size}, device_id_type=MESH)

    pl.semaphore_wait(barrier, len(fiber_steps) + x_size + y_size - 2)

    my_rows = pl.ds(pl.multiple_of(fiber * rows, rows), rows)
    copies = []
    for index, (z_step, core_step) in enumerate(fiber_steps):
        peer = fiber_at(z_step, core_step)
        copy = pltpu.make_async_remote_copy(
            src_ref=outgoing.at[peer], dst_ref=columns_ref.at[my_rows],
            send_sem=a2a_send.at[index], recv_sem=a2a_recv.at[index],
            device_id={"af": peer}, device_id_type=MESH,
        )
        copy.start()
        copies.append(copy)
    columns_ref[my_rows, :] = outgoing[fiber]
    for copy in copies:
        copy.wait()

    scale = 1.0 / (block_cols * fibers * x_size * y_size)
    pairs = [(i, j) for i in range(4) for j in range(i + 1)]
    per_core = len(pairs) // 2

    def gram_blocks(owner):
        for index in range(per_core):
            (i0, j0), (i1, j1) = pairs[index], pairs[per_core + index]
            i = i0 + owner * (i1 - i0)
            j = j0 + owner * (j1 - j0)
            left = columns_ref[pl.ds(pl.multiple_of(i * TILE, TILE), TILE), :]
            right = columns_ref[pl.ds(pl.multiple_of(j * TILE, TILE), TILE), :]
            product = lax.dot_general(left, right, (((1,), (1,)), ((), ())), preferred_element_type=jnp.float32)
            at = pl.multiple_of(owner * half + index * TILE, TILE)
            part[pl.ds(at, TILE), :] = product * scale

    other = (core + 1) % 2
    gram_blocks(other)
    pair = pltpu.make_async_remote_copy(
        src_ref=part.at[pl.ds(pl.multiple_of(other * half, half), half)], dst_ref=pair_land,
        send_sem=pair_send, recv_sem=pair_recv,
        device_id={"af": fiber_at(0, 1)}, device_id_type=MESH,
    )
    pair.start()
    gram_blocks(core)
    pair.wait()
    my_half = pl.ds(pl.multiple_of(core * half, half), half)
    pair_sum[...] = part[my_half, :] + pair_land[...]

    copies = []
    for step in ring_offsets(x_size):
        peer = (x + step) % x_size
        copy = pltpu.make_async_remote_copy(
            src_ref=pair_sum.at[pl.ds(pl.multiple_of(peer * x_rows, x_rows), x_rows)], dst_ref=x_land.at[step - 1],
            send_sem=x_send.at[step - 1], recv_sem=x_recv.at[step - 1],
            device_id={"gy": peer}, device_id_type=MESH,
        )
        copy.start()
        copies.append(copy)
    for copy in copies:
        copy.wait()
    total = pair_sum[pl.ds(pl.multiple_of(x * x_rows, x_rows), x_rows), :]
    for step in range(1, x_size):
        total = total + x_land[step - 1]
    x_sum[...] = total

    def tile_start(owner):
        return (owner * (x_rows // 8) // y_size) * 8

    copies = []
    for step in ring_offsets(y_size):
        peer = (y + step) % y_size
        copy = pltpu.make_async_remote_copy(
            src_ref=x_sum.at[pl.ds(pl.multiple_of(tile_start(peer), 8), y_rows)], dst_ref=y_land.at[step - 1],
            send_sem=y_send.at[step - 1], recv_sem=y_recv.at[step - 1],
            device_id={"gz": peer}, device_id_type=MESH,
        )
        copy.start()
        copies.append(copy)
    for copy in copies:
        copy.wait()
    total = x_sum[pl.ds(pl.multiple_of(tile_start(y), 8), y_rows), :]
    for step in range(1, y_size):
        total = total + y_land[step - 1]

    z_land[z] = total
    copies = []
    for step in ring_offsets(z_size):
        peer = fiber_at(step, 0)
        copy = pltpu.make_async_remote_copy(
            src_ref=z_land.at[z], dst_ref=z_land.at[z],
            send_sem=z_send.at[step - 1], recv_sem=z_recv.at[step - 1],
            device_id={"af": peer}, device_id_type=MESH,
        )
        copy.start()
        copies.append(copy)
    for copy in copies:
        copy.wait()
    total = z_land[0]
    for index in range(1, z_size):
        total = total + z_land[index]

    y_gather[y] = total
    copies = []
    for step in ring_offsets(y_size):
        peer = (y + step) % y_size
        copy = pltpu.make_async_remote_copy(
            src_ref=y_gather.at[y], dst_ref=y_gather.at[y],
            send_sem=yg_send.at[step - 1], recv_sem=yg_recv.at[step - 1],
            device_id={"gz": peer}, device_id_type=MESH,
        )
        copy.start()
        copies.append(copy)
    for copy in copies:
        copy.wait()
    my_x = pl.multiple_of(x * x_rows, x_rows)
    for owner in range(y_size):
        first = tile_start(owner)
        last = tile_start(owner + 1) if owner + 1 < y_size else x_rows
        x_gather[pl.ds(pl.multiple_of(my_x + first, 8), last - first), :] = y_gather[owner, : last - first, :]

    copies = []
    mine = pl.ds(my_x, x_rows)
    for step in ring_offsets(x_size):
        peer = (x + step) % x_size
        copy = pltpu.make_async_remote_copy(
            src_ref=x_gather.at[mine], dst_ref=x_gather.at[mine],
            send_sem=xg_send.at[step - 1], recv_sem=xg_recv.at[step - 1],
            device_id={"gy": peer}, device_id_type=MESH,
        )
        copy.start()
        copies.append(copy)
    for copy in copies:
        copy.wait()

    final = pltpu.make_async_remote_copy(
        src_ref=x_gather, dst_ref=gram_ref.at[my_half],
        send_sem=final_send, recv_sem=final_recv,
        device_id={"af": fiber_at(0, 1)}, device_id_type=MESH,
    )
    final.start()
    gram_ref[my_half, :] = x_gather[...]
    final.wait()


def exchange(arranged):
    sizes = (lax.axis_size("af"), lax.axis_size("gy"), lax.axis_size("gz"))
    fibers, x_size, y_size = sizes
    z_size = fibers // 2
    rows, block_cols = arranged.shape[1:]
    all_rows = rows * fibers
    half = 5 * TILE
    x_rows = half // x_size
    y_rows = max(
        (((p + 1) * (x_rows // 8)) // y_size - (p * (x_rows // 8)) // y_size) for p in range(y_size)
    ) * 8
    dma = pltpu.SemaphoreType.DMA
    f32, bf16 = jnp.float32, jnp.bfloat16
    return pl.pallas_call(
        functools.partial(exchange_kernel, sizes),
        out_shape=(
            jax.ShapeDtypeStruct((all_rows, block_cols), bf16),
            jax.ShapeDtypeStruct((2 * half, TILE), f32),
        ),
        in_specs=[pl.BlockSpec(memory_space=pltpu.VMEM)],
        out_specs=[pl.BlockSpec(memory_space=pltpu.VMEM)] * 2,
        scratch_shapes=[
            pltpu.VMEM((2 * half, TILE), f32),
            pltpu.VMEM((half, TILE), f32),
            pltpu.VMEM((half, TILE), f32),
            pltpu.VMEM((x_size - 1, x_rows, TILE), f32),
            pltpu.VMEM((x_rows, TILE), f32),
            pltpu.VMEM((y_size - 1, y_rows, TILE), f32),
            pltpu.VMEM((z_size, y_rows, TILE), f32),
            pltpu.VMEM((y_size, y_rows, TILE), f32),
            pltpu.VMEM((half, TILE), f32),
            dma((fibers - 1,)), dma((fibers - 1,)), dma, dma,
            dma((x_size - 1,)), dma((x_size - 1,)), dma((y_size - 1,)), dma((y_size - 1,)),
            dma((z_size - 1,)), dma((z_size - 1,)),
            dma((y_size - 1,)), dma((y_size - 1,)), dma((x_size - 1,)), dma((x_size - 1,)), dma, dma,
        ],
        compiler_params=pltpu.CompilerParams(collective_id=0, has_side_effects=True, vmem_limit_bytes=32 << 20),
    )(arranged)


exact_mode = lax.Precision.HIGHEST


def orthonormal(matrix):
    inner_prod = jnp.dot(matrix.T, matrix, precision=exact_mode)
    factor = jnp.linalg.cholesky(inner_prod)
    return lax.linalg.triangular_solve(
        factor, matrix, left_side=False, lower=True, transpose_a=True
    )


def on_device(slab, block_owner, basis_init):
    fibers = lax.axis_size("af")
    labels = jnp.arange(fibers, dtype=jnp.int32)
    onehot = (block_owner.reshape(fibers)[:, None] == labels[None, :]).astype(jnp.int32)
    source = jnp.sum(onehot * labels[:, None], axis=0)
    pieces = slab.reshape(slab.shape[0], fibers, -1)
    columns, packed = exchange(jnp.take(pieces, source, axis=1).transpose(1, 0, 2))
    blocks = packed.reshape(10, TILE, TILE)
    grid = {}
    index = 0
    for i in range(4):
        for j in range(i + 1):
            grid[i, j] = blocks[index]
            grid[j, i] = blocks[index] if i == j else blocks[index].T
            index += 1
    gram = jnp.concatenate([jnp.concatenate([grid[i, j] for j in range(4)], axis=1) for i in range(4)], axis=0)
    triangle = jnp.linalg.cholesky(gram, symmetrize_input=False)
    basis = basis_init
    for sweep in range(ITERS):
        half_basis = orthonormal(jnp.dot(triangle.T, basis, precision=exact_mode))
        basis = orthonormal(jnp.dot(triangle, half_basis, precision=exact_mode))
    narrow = basis.astype(jnp.bfloat16)
    core = jnp.dot(narrow.T, columns, preferred_element_type=jnp.float32).astype(jnp.bfloat16)
    return (triangle, basis, core)


def solution(mesh):
    placed = (P("af", ("gy", "gz")), P("gy", "gz", None), P())
    return jax.shard_map(
        on_device,
        mesh=mesh,
        in_specs=placed,
        out_specs=(P(), P(), P(None, ("gy", "gz", "af"))),
        check_vma=False,
    )
```

```python
import functools
import jax
import jax.numpy as jnp
from jax import lax
from jax.experimental import pallas as pl
from jax.experimental.pallas import tpu as pltpu
from jax.sharding import PartitionSpec as P

TILE = 128
STRIP = 8
exact_mode = lax.Precision.HIGHEST
MESH = pl.DeviceIdType.MESH


def ring_offsets(size):
    return sorted(range(1, size), key=lambda step: -min(step, size - step))


def exchange_kernel(
    sizes, outgoing, columns_ref, gram_ref,
    part, pair_land, pair_sum, x_land, x_sum, y_land, z_land, y_gather, x_gather,
    a2a_send, a2a_recv, pair_send, pair_recv, x_send, x_recv, y_send, y_recv, z_send, z_recv,
    yg_send, yg_recv, xg_send, xg_recv, final_send, final_recv,
):
    fibers, x_size, y_size = sizes
    z_size = fibers // 2
    rows, block_cols = outgoing.shape[1:]
    fiber = lax.axis_index("af")
    x = lax.axis_index("gy")
    y = lax.axis_index("gz")
    z, core = fiber // 2, fiber % 2
    half = pair_sum.shape[0]
    x_rows = x_sum.shape[0]
    y_rows = y_land.shape[1]

    def fiber_at(z_step, core_step):
        return ((z + z_step) % z_size) * 2 + (core + core_step) % 2

    fiber_steps = [(s, c) for s in ring_offsets(z_size) for c in (0, 1)] + [(0, 1)]
    barrier = pltpu.get_barrier_semaphore()
    for z_step, core_step in fiber_steps:
        pl.semaphore_signal(barrier, inc=1, device_id={"af": fiber_at(z_step, core_step)}, device_id_type=MESH)
    for step in range(1, y_size):
        pl.semaphore_signal(barrier, inc=1, device_id={"gz": (y + step) % y_size}, device_id_type=MESH)
    for step in range(1, x_size):
        pl.semaphore_signal(barrier, inc=1, device_id={"gy": (x + step) % x_size}, device_id_type=MESH)

    pl.semaphore_wait(barrier, len(fiber_steps) + x_size + y_size - 2)

    my_rows = pl.ds(pl.multiple_of(fiber * rows, rows), rows)
    copies = []
    for index, (z_step, core_step) in enumerate(fiber_steps):
        peer = fiber_at(z_step, core_step)
        copy = pltpu.make_async_remote_copy(
            src_ref=outgoing.at[peer], dst_ref=columns_ref.at[my_rows],
            send_sem=a2a_send.at[index], recv_sem=a2a_recv.at[index],
            device_id={"af": peer}, device_id_type=MESH,
        )
        copy.start()
        copies.append(copy)
    columns_ref[my_rows, :] = outgoing[fiber]
    for copy in copies:
        copy.wait()

    scale = 1.0 / (block_cols * fibers * x_size * y_size)
    pairs = [(i, j) for i in range(4) for j in range(i + 1)]
    per_core = len(pairs) // 2

    def gram_blocks(owner):
        for index in range(per_core):
            (i0, j0), (i1, j1) = pairs[index], pairs[per_core + index]
            i = i0 + owner * (i1 - i0)
            j = j0 + owner * (j1 - j0)
            left = columns_ref[pl.ds(pl.multiple_of(i * TILE, TILE), TILE), :]
            right = columns_ref[pl.ds(pl.multiple_of(j * TILE, TILE), TILE), :]
            product = lax.dot_general(left, right, (((1,), (1,)), ((), ())), preferred_element_type=jnp.float32)
            at = pl.multiple_of(owner * half + index * TILE, TILE)
            part[pl.ds(at, TILE), :] = product * scale

    other = (core + 1) % 2
    gram_blocks(other)
    pair = pltpu.make_async_remote_copy(
        src_ref=part.at[pl.ds(pl.multiple_of(other * half, half), half)], dst_ref=pair_land,
        send_sem=pair_send, recv_sem=pair_recv,
        device_id={"af": fiber_at(0, 1)}, device_id_type=MESH,
    )
    pair.start()
    gram_blocks(core)
    pair.wait()
    my_half = pl.ds(pl.multiple_of(core * half, half), half)
    pair_sum[...] = part[my_half, :] + pair_land[...]

    copies = []
    for step in ring_offsets(x_size):
        peer = (x + step) % x_size
        copy = pltpu.make_async_remote_copy(
            src_ref=pair_sum.at[pl.ds(pl.multiple_of(peer * x_rows, x_rows), x_rows)], dst_ref=x_land.at[step - 1],
            send_sem=x_send.at[step - 1], recv_sem=x_recv.at[step - 1],
            device_id={"gy": peer}, device_id_type=MESH,
        )
        copy.start()
        copies.append(copy)
    for copy in copies:
        copy.wait()
    total = pair_sum[pl.ds(pl.multiple_of(x * x_rows, x_rows), x_rows), :]
    for step in range(1, x_size):
        total = total + x_land[step - 1]
    x_sum[...] = total

    def tile_start(owner):
        return (owner * (x_rows // 8) // y_size) * 8

    copies = []
    for step in ring_offsets(y_size):
        peer = (y + step) % y_size
        copy = pltpu.make_async_remote_copy(
            src_ref=x_sum.at[pl.ds(pl.multiple_of(tile_start(peer), 8), y_rows)], dst_ref=y_land.at[step - 1],
            send_sem=y_send.at[step - 1], recv_sem=y_recv.at[step - 1],
            device_id={"gz": peer}, device_id_type=MESH,
        )
        copy.start()
        copies.append(copy)
    for copy in copies:
        copy.wait()
    total = x_sum[pl.ds(pl.multiple_of(tile_start(y), 8), y_rows), :]
    for step in range(1, y_size):
        total = total + y_land[step - 1]

    z_land[z] = total
    copies = []
    for step in ring_offsets(z_size):
        peer = fiber_at(step, 0)
        copy = pltpu.make_async_remote_copy(
            src_ref=z_land.at[z], dst_ref=z_land.at[z],
            send_sem=z_send.at[step - 1], recv_sem=z_recv.at[step - 1],
            device_id={"af": peer}, device_id_type=MESH,
        )
        copy.start()
        copies.append(copy)
    for copy in copies:
        copy.wait()
    total = z_land[0]
    for index in range(1, z_size):
        total = total + z_land[index]

    y_gather[y] = total
    copies = []
    for step in ring_offsets(y_size):
        peer = (y + step) % y_size
        copy = pltpu.make_async_remote_copy(
            src_ref=y_gather.at[y], dst_ref=y_gather.at[y],
            send_sem=yg_send.at[step - 1], recv_sem=yg_recv.at[step - 1],
            device_id={"gz": peer}, device_id_type=MESH,
        )
        copy.start()
        copies.append(copy)
    for copy in copies:
        copy.wait()
    my_x = pl.multiple_of(x * x_rows, x_rows)
    for owner in range(y_size):
        first = tile_start(owner)
        last = tile_start(owner + 1) if owner + 1 < y_size else x_rows
        x_gather[pl.ds(pl.multiple_of(my_x + first, 8), last - first), :] = y_gather[owner, : last - first, :]

    copies = []
    mine = pl.ds(my_x, x_rows)
    for step in ring_offsets(x_size):
        peer = (x + step) % x_size
        copy = pltpu.make_async_remote_copy(
            src_ref=x_gather.at[mine], dst_ref=x_gather.at[mine],
            send_sem=xg_send.at[step - 1], recv_sem=xg_recv.at[step - 1],
            device_id={"gy": peer}, device_id_type=MESH,
        )
        copy.start()
        copies.append(copy)
    for copy in copies:
        copy.wait()

    final = pltpu.make_async_remote_copy(
        src_ref=x_gather, dst_ref=gram_ref.at[my_half],
        send_sem=final_send, recv_sem=final_recv,
        device_id={"af": fiber_at(0, 1)}, device_id_type=MESH,
    )
    final.start()
    gram_ref[my_half, :] = x_gather[...]
    final.wait()


def exchange(arranged):
    sizes = (lax.axis_size("af"), lax.axis_size("gy"), lax.axis_size("gz"))
    fibers, x_size, y_size = sizes
    z_size = fibers // 2
    rows, block_cols = arranged.shape[1:]
    all_rows = rows * fibers
    half = 5 * TILE
    x_rows = half // x_size
    y_rows = max(
        (((p + 1) * (x_rows // 8)) // y_size - (p * (x_rows // 8)) // y_size) for p in range(y_size)
    ) * 8
    dma = pltpu.SemaphoreType.DMA
    f32, bf16 = jnp.float32, jnp.bfloat16
    return pl.pallas_call(
        functools.partial(exchange_kernel, sizes),
        out_shape=(
            jax.ShapeDtypeStruct((all_rows, block_cols), bf16),
            jax.ShapeDtypeStruct((2 * half, TILE), f32),
        ),
        in_specs=[pl.BlockSpec(memory_space=pltpu.VMEM)],
        out_specs=[pl.BlockSpec(memory_space=pltpu.VMEM)] * 2,
        scratch_shapes=[
            pltpu.VMEM((2 * half, TILE), f32),
            pltpu.VMEM((half, TILE), f32),
            pltpu.VMEM((half, TILE), f32),
            pltpu.VMEM((x_size - 1, x_rows, TILE), f32),
            pltpu.VMEM((x_rows, TILE), f32),
            pltpu.VMEM((y_size - 1, y_rows, TILE), f32),
            pltpu.VMEM((z_size, y_rows, TILE), f32),
            pltpu.VMEM((y_size, y_rows, TILE), f32),
            pltpu.VMEM((half, TILE), f32),
            dma((fibers - 1,)), dma((fibers - 1,)), dma, dma,
            dma((x_size - 1,)), dma((x_size - 1,)), dma((y_size - 1,)), dma((y_size - 1,)),
            dma((z_size - 1,)), dma((z_size - 1,)),
            dma((y_size - 1,)), dma((y_size - 1,)), dma((x_size - 1,)), dma((x_size - 1,)), dma, dma,
        ],
        compiler_params=pltpu.CompilerParams(collective_id=0, has_side_effects=True, vmem_limit_bytes=32 << 20),
    )(arranged)


def eliminate_strip(work, final, scales, first):
    f32 = jnp.float32
    shape = (STRIP, TILE)
    lane = lax.broadcasted_iota(jnp.int32, shape, 1)
    sub = lax.broadcasted_iota(jnp.int32, shape, 0)
    strip = work[pl.ds(first, STRIP), :]
    rolled = pltpu.roll(strip, TILE - first, 1)
    heads = [jnp.broadcast_to(rolled[:, t : t + 1], shape) for t in range(STRIP)]
    full = strip
    down = strip
    scale = jnp.zeros(shape, f32)
    for t in range(STRIP):
        head = heads[t]
        pivot = jnp.broadcast_to(head[t : t + 1, :], shape)
        inverse = 1.0 / pivot
        scale = jnp.where(sub == t, lax.rsqrt(pivot), scale)
        factor = head * inverse
        here = lane == first + t
        row = jnp.where(here, 1.0, jnp.broadcast_to(full[t : t + 1, :], shape))
        full = jnp.where(sub == t, row * inverse, jnp.where(here, 0.0, full) - factor * row)
        drow = jnp.where(here, 1.0, jnp.broadcast_to(down[t : t + 1, :], shape))
        down = jnp.where(sub > t, jnp.where(here, 0.0, down) - factor * drow, down)
        for u in range(t + 1, STRIP):
            line = jnp.broadcast_to(heads[u][t : t + 1, :], shape)
            heads[u] = jnp.where(sub == t, line * inverse, heads[u] - factor * line)
    final[pl.ds(first, STRIP), :] = down * scale
    scales[pl.ds(first, STRIP), :] = scale
    return full


def strip_update(work, full, first):
    lane = lax.broadcasted_iota(jnp.int32, (TILE, TILE), 1)
    sub = lax.broadcasted_iota(jnp.int32, (TILE, TILE), 0)
    rows = work[...]
    own = (lane >= first) & (lane < first + STRIP)
    below = sub >= first + STRIP
    head = pltpu.roll(rows, TILE - first, 1)[:, :STRIP]
    update = jnp.dot(head, full, precision=exact_mode, preferred_element_type=jnp.float32)
    work[...] = jnp.where(below, jnp.where(own, 0.0, rows) - update, rows)


def factor_both(works, finals, scales):
    @pl.loop(0, TILE // STRIP)
    def _(index):
        first = pl.multiple_of(index * STRIP, STRIP)
        fulls = [eliminate_strip(w, f, s, first) for w, f, s in zip(works, finals, scales)]
        for work, full in zip(works, fulls):
            strip_update(work, full, first)


def inverse_of(final, scales):
    lane = lax.broadcasted_iota(jnp.int32, (TILE, TILE), 1)
    sub = lax.broadcasted_iota(jnp.int32, (TILE, TILE), 0)
    return jnp.where(lane < sub, final[...], jnp.where(lane == sub, scales[...], 0.0))


def upper_of(final):
    lane = lax.broadcasted_iota(jnp.int32, (TILE, TILE), 1)
    sub = lax.broadcasted_iota(jnp.int32, (TILE, TILE), 0)
    return jnp.where(lane >= sub, final[...], 0.0)


def dot_exact(a, b, dims):
    return lax.dot_general(a, b, (dims, ((), ())), precision=exact_mode, preferred_element_type=jnp.float32)


NN, NT, TN = ((1,), (0,)), ((1,), (1,)), ((0,), (0,))


def factor_kernel(
    packed_ref, start_ref, columns_ref, triangle_ref, basis_ref, core_ref,
    gram, trail, product, work_a, work_b, final_a, final_b, scale_a, scale_b,
):
    count = 4
    spot = lambda i, j: pl.ds((i * (i + 1) // 2 + j) * TILE, TILE)
    at = lambda i: pl.ds(i * TILE, TILE)
    for i in range(count):
        for j in range(i + 1):
            block = packed_ref[spot(i, j), :]
            gram[at(i), at(j)] = block
            trail[at(i), at(j)] = block
            if i != j:
                gram[at(j), at(i)] = block.T
                triangle_ref[at(j), at(i)] = jnp.zeros((TILE, TILE), jnp.float32)
    start = start_ref[...]
    image = dot_exact(gram[...], start, NN)
    product[...] = image
    work_b[...] = dot_exact(start, image, TN)
    for k in range(count):
        work_a[...] = trail[at(k), at(k)]
        factor_both((work_a, work_b), (final_a, final_b), (scale_a, scale_b))
        turn = inverse_of(final_b, scale_b)
        image = dot_exact(product[...], turn, NT)
        if k == 0 or k == 2:
            product[...] = image
            work_b[...] = dot_exact(image, image, TN)
        elif k == 1:
            moved = dot_exact(gram[...], image, NN)
            product[...] = moved
            work_b[...] = dot_exact(image, moved, TN)
        else:
            basis_ref[...] = image
            core_ref[...] = lax.dot_general(
                image.astype(jnp.bfloat16), columns_ref[...], (TN, ((), ())), preferred_element_type=jnp.float32
            ).astype(jnp.bfloat16)
        triangle_ref[at(k), at(k)] = upper_of(final_a).T
        if k + 1 < count:
            rest = pl.ds((k + 1) * TILE, (count - 1 - k) * TILE)
            lower = dot_exact(trail[rest, at(k)], inverse_of(final_a, scale_a), NT)
            triangle_ref[rest, at(k)] = lower
            for j in range(k + 1, count):
                tail = pl.ds(j * TILE, (count - j) * TILE)
                skip = (j - k - 1) * TILE
                trail[tail, at(j)] = trail[tail, at(j)] - dot_exact(lower[skip:], lower[skip : skip + TILE], NT)


def factor(packed, start, columns):
    f32 = jnp.float32
    rows, rank = start.shape
    square = pltpu.VMEM((TILE, TILE), f32)
    return pl.pallas_call(
        factor_kernel,
        out_shape=(
            jax.ShapeDtypeStruct((rows, rows), f32),
            jax.ShapeDtypeStruct((rows, rank), f32),
            jax.ShapeDtypeStruct((rank, columns.shape[1]), jnp.bfloat16),
        ),
        in_specs=[pl.BlockSpec(memory_space=pltpu.VMEM)] * 3,
        out_specs=[pl.BlockSpec(memory_space=pltpu.VMEM)] * 3,
        scratch_shapes=[
            pltpu.VMEM((rows, rows), f32), pltpu.VMEM((rows, rows), f32), pltpu.VMEM((rows, rank), f32),
            square, square, square, square, square, square,
        ],
        compiler_params=pltpu.CompilerParams(vmem_limit_bytes=32 << 20),
    )(packed, start, columns)


def on_device(slab, block_owner, basis_init):
    fibers = lax.axis_size("af")
    labels = jnp.arange(fibers, dtype=jnp.int32)
    onehot = (block_owner.reshape(fibers)[:, None] == labels[None, :]).astype(jnp.int32)
    source = jnp.sum(onehot * labels[:, None], axis=0)
    pieces = slab.reshape(slab.shape[0], fibers, -1)
    columns, packed = exchange(jnp.take(pieces, source, axis=1).transpose(1, 0, 2))
    return factor(packed, basis_init, columns)


def solution(mesh):
    placed = (P("af", ("gy", "gz")), P("gy", "gz", None), P())
    return jax.shard_map(
        on_device,
        mesh=mesh,
        in_specs=placed,
        out_specs=(P(), P(), P(None, ("gy", "gz", "af"))),
        check_vma=False,
    )
```

```python
import functools
import jax
import jax.numpy as jnp
from jax import lax
from jax.experimental import pallas as pl
from jax.experimental.pallas import tpu as pltpu
from jax.sharding import PartitionSpec as P

TILE = 128
STRIP = 8
exact_mode = lax.Precision.HIGHEST
MESH = pl.DeviceIdType.MESH


def ring_offsets(size):
    return sorted(range(1, size), key=lambda step: -min(step, size - step))


def exchange_kernel(
    sizes, outgoing, columns_ref, pieces_ref,
    part, pair_land, pair_sum, x_land, x_sum, y_land, z_land,
    a2a_send, a2a_recv, pair_send, pair_recv, x_send, x_recv, y_send, y_recv, z_send, z_recv,
    yg_send, yg_recv, xg_send, xg_recv, final_send, final_recv,
):
    fibers, x_size, y_size = sizes
    z_size = fibers // 2
    rows, block_cols = outgoing.shape[1:]
    fiber = lax.axis_index("af")
    x = lax.axis_index("gy")
    y = lax.axis_index("gz")
    z, core = fiber // 2, fiber % 2
    half = pair_sum.shape[0]
    x_rows = x_sum.shape[0]
    y_rows = y_land.shape[1]

    def fiber_at(z_step, core_step):
        return ((z + z_step) % z_size) * 2 + (core + core_step) % 2

    fiber_steps = [(s, c) for s in ring_offsets(z_size) for c in (0, 1)] + [(0, 1)]
    barrier = pltpu.get_barrier_semaphore()
    for z_step, core_step in fiber_steps:
        pl.semaphore_signal(barrier, inc=1, device_id={"af": fiber_at(z_step, core_step)}, device_id_type=MESH)
    for step in range(1, y_size):
        pl.semaphore_signal(barrier, inc=1, device_id={"gz": (y + step) % y_size}, device_id_type=MESH)
    for step in range(1, x_size):
        pl.semaphore_signal(barrier, inc=1, device_id={"gy": (x + step) % x_size}, device_id_type=MESH)

    pl.semaphore_wait(barrier, len(fiber_steps) + x_size + y_size - 2)

    my_rows = pl.ds(pl.multiple_of(fiber * rows, rows), rows)
    copies = []
    for index, (z_step, core_step) in enumerate(fiber_steps):
        peer = fiber_at(z_step, core_step)
        copy = pltpu.make_async_remote_copy(
            src_ref=outgoing.at[peer], dst_ref=columns_ref.at[my_rows],
            send_sem=a2a_send.at[index], recv_sem=a2a_recv.at[index],
            device_id={"af": peer}, device_id_type=MESH,
        )
        copy.start()
        copies.append(copy)
    columns_ref[my_rows, :] = outgoing[fiber]
    for copy in copies:
        copy.wait()

    scale = 1.0 / (block_cols * fibers * x_size * y_size)
    pairs = [(i, j) for i in range(4) for j in range(i + 1)]
    per_core = len(pairs) // 2

    def gram_blocks(owner):
        for index in range(per_core):
            (i0, j0), (i1, j1) = pairs[index], pairs[per_core + index]
            i = i0 + owner * (i1 - i0)
            j = j0 + owner * (j1 - j0)
            left = columns_ref[pl.ds(pl.multiple_of(i * TILE, TILE), TILE), :]
            right = columns_ref[pl.ds(pl.multiple_of(j * TILE, TILE), TILE), :]
            product = lax.dot_general(left, right, (((1,), (1,)), ((), ())), preferred_element_type=jnp.float32)
            at = pl.multiple_of(owner * half + index * TILE, TILE)
            part[pl.ds(at, TILE), :] = product * scale

    other = (core + 1) % 2
    gram_blocks(other)
    pair = pltpu.make_async_remote_copy(
        src_ref=part.at[pl.ds(pl.multiple_of(other * half, half), half)], dst_ref=pair_land,
        send_sem=pair_send, recv_sem=pair_recv,
        device_id={"af": fiber_at(0, 1)}, device_id_type=MESH,
    )
    pair.start()
    gram_blocks(core)
    pair.wait()
    my_half = pl.ds(pl.multiple_of(core * half, half), half)
    pair_sum[...] = part[my_half, :] + pair_land[...]

    copies = []
    for step in ring_offsets(x_size):
        peer = (x + step) % x_size
        copy = pltpu.make_async_remote_copy(
            src_ref=pair_sum.at[pl.ds(pl.multiple_of(peer * x_rows, x_rows), x_rows)], dst_ref=x_land.at[step - 1],
            send_sem=x_send.at[step - 1], recv_sem=x_recv.at[step - 1],
            device_id={"gy": peer}, device_id_type=MESH,
        )
        copy.start()
        copies.append(copy)
    for copy in copies:
        copy.wait()
    total = pair_sum[pl.ds(pl.multiple_of(x * x_rows, x_rows), x_rows), :]
    for step in range(1, x_size):
        total = total + x_land[step - 1]
    x_sum[...] = total

    def tile_start(owner):
        return (owner * (x_rows // 8) // y_size) * 8

    copies = []
    for step in ring_offsets(y_size):
        peer = (y + step) % y_size
        copy = pltpu.make_async_remote_copy(
            src_ref=x_sum.at[pl.ds(pl.multiple_of(tile_start(peer), 8), y_rows)], dst_ref=y_land.at[step - 1],
            send_sem=y_send.at[step - 1], recv_sem=y_recv.at[step - 1],
            device_id={"gz": peer}, device_id_type=MESH,
        )
        copy.start()
        copies.append(copy)
    for copy in copies:
        copy.wait()
    total = x_sum[pl.ds(pl.multiple_of(tile_start(y), 8), y_rows), :]
    for step in range(1, y_size):
        total = total + y_land[step - 1]

    z_land[z] = total
    copies = []
    for step in ring_offsets(z_size):
        peer = fiber_at(step, 0)
        copy = pltpu.make_async_remote_copy(
            src_ref=z_land.at[z], dst_ref=z_land.at[z],
            send_sem=z_send.at[step - 1], recv_sem=z_recv.at[step - 1],
            device_id={"af": peer}, device_id_type=MESH,
        )
        copy.start()
        copies.append(copy)
    for copy in copies:
        copy.wait()
    total = z_land[0]
    for index in range(1, z_size):
        total = total + z_land[index]

    pieces_ref[core, x, y] = total
    near = sorted(range(1, y_size), key=lambda step: min(step, y_size - step))
    sent = []

    def send(where, sems, index, target):
        slot = pieces_ref.at[where]
        copy = pltpu.make_async_remote_copy(
            src_ref=slot, dst_ref=slot, send_sem=sems[0].at[index], recv_sem=sems[1].at[index],
            device_id=target, device_id_type=MESH,
        )
        copy.start()
        sent.append(copy)

    def wait_for(where, sems, index, target):
        slot = pieces_ref.at[where]
        pltpu.make_async_remote_copy(
            src_ref=slot, dst_ref=slot, send_sem=sems[0].at[index], recv_sem=sems[1].at[index],
            device_id=target, device_id_type=MESH,
        ).wait_recv()

    partner = {"af": fiber_at(0, 1)}
    other = (core + 1) % 2
    for step in reversed(near):
        send((core, x, y), (yg_send, yg_recv), step - 1, {"gz": (y + step) % y_size})
    for place in range(y_size):
        owner = y
        if place > 0:
            step = near[place - 1]
            owner = (y + y_size - step) % y_size
            wait_for((core, x, owner), (yg_send, yg_recv), step - 1, {"gz": owner})
        for step in ring_offsets(x_size):
            send((core, x, owner), (xg_send, xg_recv), (step - 1) * y_size + place, {"gy": (x + step) % x_size})
        send((core, x, owner), (final_send, final_recv), place, partner)
    for place in range(y_size):
        owner = (y + y_size - near[place - 1]) % y_size if place > 0 else y
        for step in sorted(range(1, x_size), key=lambda step: min(step, x_size - step)):
            origin = (x + x_size - step) % x_size
            wait_for((core, origin, owner), (xg_send, xg_recv), (step - 1) * y_size + place, {"gy": origin})
            send((core, origin, owner), (final_send, final_recv), step * y_size + place, partner)
    for place in range(y_size):
        owner = (y + y_size - near[place - 1]) % y_size if place > 0 else y
        for step in range(x_size):
            origin = (x + x_size - step) % x_size
            wait_for((other, origin, owner), (final_send, final_recv), step * y_size + place, partner)
    for copy in sent:
        copy.wait_send()


def arrange_kernel(owner_ref, slab_ref, out_ref):
    fibers, _, block_cols = out_ref.shape
    for target in range(fibers):
        source = jnp.int32(0)
        for block in range(1, fibers):
            source = source + jnp.where(owner_ref[block] == target, block, 0)
        start = pl.multiple_of(source * block_cols, block_cols)
        out_ref[target] = slab_ref[:, pl.ds(start, block_cols)]


def arrange(owners, slab):
    fibers = owners.shape[0]
    rows, width = slab.shape
    return pl.pallas_call(
        arrange_kernel,
        out_shape=jax.ShapeDtypeStruct((fibers, rows, width // fibers), slab.dtype),
        in_specs=[pl.BlockSpec(memory_space=pltpu.SMEM), pl.BlockSpec(memory_space=pltpu.VMEM)],
        out_specs=pl.BlockSpec(memory_space=pltpu.VMEM),
        compiler_params=pltpu.CompilerParams(vmem_limit_bytes=16 << 20),
    )(owners, slab)


def exchange(arranged):
    sizes = (lax.axis_size("af"), lax.axis_size("gy"), lax.axis_size("gz"))
    fibers, x_size, y_size = sizes
    z_size = fibers // 2
    rows, block_cols = arranged.shape[1:]
    all_rows = rows * fibers
    half = 5 * TILE
    x_rows = half // x_size
    y_rows = max(
        (((p + 1) * (x_rows // 8)) // y_size - (p * (x_rows // 8)) // y_size) for p in range(y_size)
    ) * 8
    dma = pltpu.SemaphoreType.DMA
    f32, bf16 = jnp.float32, jnp.bfloat16
    return pl.pallas_call(
        functools.partial(exchange_kernel, sizes),
        out_shape=(
            jax.ShapeDtypeStruct((all_rows, block_cols), bf16),
            jax.ShapeDtypeStruct((2, x_size, y_size, y_rows, TILE), f32),
        ),
        in_specs=[pl.BlockSpec(memory_space=pltpu.VMEM)],
        out_specs=[pl.BlockSpec(memory_space=pltpu.VMEM)] * 2,
        scratch_shapes=[
            pltpu.VMEM((2 * half, TILE), f32),
            pltpu.VMEM((half, TILE), f32),
            pltpu.VMEM((half, TILE), f32),
            pltpu.VMEM((x_size - 1, x_rows, TILE), f32),
            pltpu.VMEM((x_rows, TILE), f32),
            pltpu.VMEM((y_size - 1, y_rows, TILE), f32),
            pltpu.VMEM((z_size, y_rows, TILE), f32),
            dma((fibers - 1,)), dma((fibers - 1,)), dma, dma,
            dma((x_size - 1,)), dma((x_size - 1,)), dma((y_size - 1,)), dma((y_size - 1,)),
            dma((z_size - 1,)), dma((z_size - 1,)),
            dma((y_size - 1,)), dma((y_size - 1,)),
            dma(((x_size - 1) * y_size,)), dma(((x_size - 1) * y_size,)),
            dma((x_size * y_size,)), dma((x_size * y_size,)),
        ],
        compiler_params=pltpu.CompilerParams(collective_id=0, has_side_effects=True, vmem_limit_bytes=32 << 20),
    )(arranged)


NN, NT, TN = ((1,), (0,)), ((1,), (1,)), ((0,), (0,))


def parts_of(a):
    f32, bf16 = jnp.float32, jnp.bfloat16
    high = a.astype(bf16).astype(f32)
    rest = a - high
    middle = rest.astype(bf16).astype(f32)
    return high, middle, rest - middle


def stacked(a, order, axis):
    parts = parts_of(a)
    return jnp.concatenate([parts[k] for k in order], axis=axis).astype(jnp.bfloat16)


LEFT, RIGHT = (0, 0, 1, 1, 0, 2), (0, 1, 0, 1, 2, 0)


def dot_exact(a, b, dims):
    (da,), (db,) = dims
    return lax.dot_general(
        stacked(a, LEFT, da), stacked(b, RIGHT, db), (dims, ((), ())), preferred_element_type=jnp.float32
    )


def eliminate_strip(work, final, scales, first):
    f32 = jnp.float32
    shape = (STRIP, TILE)
    lane = lax.broadcasted_iota(jnp.int32, shape, 1)
    sub = lax.broadcasted_iota(jnp.int32, shape, 0)
    strip = work[pl.ds(first, STRIP), :]
    heads = [
        jnp.take_along_axis(strip, jnp.full(shape, first + t, jnp.int32), axis=1) for t in range(STRIP)
    ]
    full = strip
    down = strip
    scale = jnp.zeros(shape, f32)
    for t in range(STRIP):
        head = heads[t]
        pivot = jnp.broadcast_to(head[t : t + 1, :], shape)
        inverse = 1.0 / pivot
        scale = jnp.where(sub == t, lax.rsqrt(pivot), scale)
        factor = head * inverse
        here = lane == first + t
        row = jnp.where(here, 1.0, jnp.broadcast_to(full[t : t + 1, :], shape))
        full = jnp.where(sub == t, row * inverse, jnp.where(here, 0.0, full) - factor * row)
        drow = jnp.where(here, 1.0, jnp.broadcast_to(down[t : t + 1, :], shape))
        down = jnp.where(sub > t, jnp.where(here, 0.0, down) - factor * drow, down)
        for u in range(t + 1, STRIP):
            line = jnp.broadcast_to(heads[u][t : t + 1, :], shape)
            heads[u] = jnp.where(sub == t, line * inverse, heads[u] - factor * line)
    final[pl.ds(first, STRIP), :] = down * scale
    scales[pl.ds(first, STRIP), :] = scale
    later = jnp.where(lane >= first + STRIP, strip, 0.0)
    return full, later


def strip_update(work, full, later, first):
    lane = lax.broadcasted_iota(jnp.int32, (TILE, TILE), 1)
    own = (lane >= first) & (lane < first + STRIP)
    update = dot_exact(later, full, TN)
    work[...] = jnp.where(own, 0.0, work[...]) - update


def factor_both(works, finals, scales):
    @pl.loop(0, TILE // STRIP)
    def _(index):
        first = pl.multiple_of(index * STRIP, STRIP)
        pieces = [eliminate_strip(w, f, s, first) for w, f, s in zip(works, finals, scales)]
        for work, (full, later) in zip(works, pieces):
            strip_update(work, full, later, first)


def inverse_of(final, scales):
    lane = lax.broadcasted_iota(jnp.int32, (TILE, TILE), 1)
    sub = lax.broadcasted_iota(jnp.int32, (TILE, TILE), 0)
    return jnp.where(lane < sub, final[...], jnp.where(lane == sub, scales[...], 0.0))


def upper_of(final):
    lane = lax.broadcasted_iota(jnp.int32, (TILE, TILE), 1)
    sub = lax.broadcasted_iota(jnp.int32, (TILE, TILE), 0)
    return jnp.where(lane >= sub, final[...], 0.0)


def factor_kernel(
    pieces_ref, start_ref, columns_ref, triangle_ref, basis_ref, core_ref,
    packed_ref, gram, trail, product, work_a, work_b, final_a, final_b, scale_a, scale_b,
):
    count = 4
    cores, x_size, y_size, _, _ = pieces_ref.shape
    tiles = packed_ref.shape[0] // 8 // cores // x_size
    for c in range(cores):
        for x in range(x_size):
            for y in range(y_size):
                first, last = tiles * y // y_size, tiles * (y + 1) // y_size
                spread = pl.ds(((c * x_size + x) * tiles + first) * 8, (last - first) * 8)
                packed_ref[spread, :] = pieces_ref[c, x, y, : (last - first) * 8, :]
    spot = lambda i, j: pl.ds((i * (i + 1) // 2 + j) * TILE, TILE)
    at = lambda i: pl.ds(i * TILE, TILE)
    for i in range(count):
        for j in range(i + 1):
            block = packed_ref[spot(i, j), :]
            gram[at(i), at(j)] = block
            trail[at(i), at(j)] = block
            if i != j:
                gram[at(j), at(i)] = block.T
                triangle_ref[at(j), at(i)] = jnp.zeros((TILE, TILE), jnp.float32)
    start = start_ref[...]
    image = dot_exact(gram[...], start, NN)
    product[...] = image
    work_b[...] = dot_exact(start, image, TN)
    for k in range(count):
        work_a[...] = trail[at(k), at(k)]
        factor_both((work_a, work_b), (final_a, final_b), (scale_a, scale_b))
        turn = inverse_of(final_b, scale_b)
        image = dot_exact(product[...], turn, NT)
        if k == 0 or k == 2:
            product[...] = image
            work_b[...] = dot_exact(image, image, TN)
        elif k == 1:
            moved = dot_exact(gram[...], image, NN)
            product[...] = moved
            work_b[...] = dot_exact(image, moved, TN)
        else:
            basis_ref[...] = image
            core_ref[...] = lax.dot_general(
                image.astype(jnp.bfloat16), columns_ref[...], (TN, ((), ())), preferred_element_type=jnp.float32
            ).astype(jnp.bfloat16)
        triangle_ref[at(k), at(k)] = upper_of(final_a).T
        if k + 1 < count:
            rest = pl.ds((k + 1) * TILE, (count - 1 - k) * TILE)
            lower = dot_exact(trail[rest, at(k)], inverse_of(final_a, scale_a), NT)
            triangle_ref[rest, at(k)] = lower
            for j in range(k + 1, count):
                tail = pl.ds(j * TILE, (count - j) * TILE)
                skip = (j - k - 1) * TILE
                trail[tail, at(j)] = trail[tail, at(j)] - dot_exact(lower[skip:], lower[skip : skip + TILE], NT)


def factor(pieces, start, columns):
    f32 = jnp.float32
    rows, rank = start.shape
    square = pltpu.VMEM((TILE, TILE), f32)
    return pl.pallas_call(
        factor_kernel,
        out_shape=(
            jax.ShapeDtypeStruct((rows, rows), f32),
            jax.ShapeDtypeStruct((rows, rank), f32),
            jax.ShapeDtypeStruct((rank, columns.shape[1]), jnp.bfloat16),
        ),
        in_specs=[pl.BlockSpec(memory_space=pltpu.VMEM)] * 3,
        out_specs=[pl.BlockSpec(memory_space=pltpu.VMEM)] * 3,
        scratch_shapes=[
            pltpu.VMEM((10 * TILE, TILE), f32), pltpu.VMEM((rows, rows), f32), pltpu.VMEM((rows, rows), f32), pltpu.VMEM((rows, rank), f32),
            square, square, square, square, square, square,
        ],
        compiler_params=pltpu.CompilerParams(vmem_limit_bytes=32 << 20),
    )(pieces, start, columns)


def on_device(slab, block_owner, basis_init):
    columns, packed = exchange(arrange(block_owner.reshape(-1), slab))
    return factor(packed, basis_init, columns)


def solution(mesh):
    placed = (P("af", ("gy", "gz")), P("gy", "gz", None), P())
    return jax.shard_map(
        on_device,
        mesh=mesh,
        in_specs=placed,
        out_specs=(P(), P(), P(None, ("gy", "gz", "af"))),
        check_vma=False,
    )
```

```python
import functools
import jax
import jax.numpy as jnp
from jax import lax
from jax.experimental import pallas as pl
from jax.experimental.pallas import tpu as pltpu
from jax.sharding import PartitionSpec as P

TILE = 128
STRIP = 8
exact_mode = lax.Precision.HIGHEST
MESH = pl.DeviceIdType.MESH


def ring_offsets(size):
    return sorted(range(1, size), key=lambda step: -min(step, size - step))


def exchange_kernel(
    sizes, outgoing, columns_ref, pieces_ref,
    part, pair_land, pair_sum, x_land, x_sum, y_land, z_land,
    a2a_send, a2a_recv, pair_send, pair_recv, x_send, x_recv, y_send, y_recv, z_send, z_recv,
    yg_send, yg_recv, xg_send, xg_recv, final_send, final_recv,
):
    fibers, x_size, y_size = sizes
    z_size = fibers // 2
    rows, block_cols = outgoing.shape[1:]
    fiber = lax.axis_index("af")
    x = lax.axis_index("gy")
    y = lax.axis_index("gz")
    z, core = fiber // 2, fiber % 2
    half = pair_sum.shape[0]
    x_rows = x_sum.shape[0]
    y_rows = y_land.shape[1]

    def fiber_at(z_step, core_step):
        return ((z + z_step) % z_size) * 2 + (core + core_step) % 2

    fiber_steps = [(0, 1)] + [(s, c) for s in reversed(ring_offsets(z_size)) for c in (0, 1)]
    barrier = pltpu.get_barrier_semaphore()
    for z_step, core_step in fiber_steps:
        pl.semaphore_signal(barrier, inc=1, device_id={"af": fiber_at(z_step, core_step)}, device_id_type=MESH)
    for step in range(1, y_size):
        pl.semaphore_signal(barrier, inc=1, device_id={"gz": (y + step) % y_size}, device_id_type=MESH)
    for step in range(1, x_size):
        pl.semaphore_signal(barrier, inc=1, device_id={"gy": (x + step) % x_size}, device_id_type=MESH)

    pl.semaphore_wait(barrier, len(fiber_steps) + x_size + y_size - 2)

    my_rows = pl.ds(pl.multiple_of(fiber * rows, rows), rows)
    copies = []
    for index, (z_step, core_step) in enumerate(fiber_steps):
        peer = fiber_at(z_step, core_step)
        copy = pltpu.make_async_remote_copy(
            src_ref=outgoing.at[peer], dst_ref=columns_ref.at[my_rows],
            send_sem=a2a_send.at[index], recv_sem=a2a_recv.at[index],
            device_id={"af": peer}, device_id_type=MESH,
        )
        copy.start()
        copies.append(copy)
    columns_ref[my_rows, :] = outgoing[fiber]
    for copy in copies:
        copy.wait()

    scale = 1.0 / (block_cols * fibers * x_size * y_size)
    pairs = [(i, j) for i in range(4) for j in range(i + 1)]
    per_core = len(pairs) // 2

    def gram_blocks(owner):
        for index in range(per_core):
            (i0, j0), (i1, j1) = pairs[index], pairs[per_core + index]
            i = i0 + owner * (i1 - i0)
            j = j0 + owner * (j1 - j0)
            left = columns_ref[pl.ds(pl.multiple_of(i * TILE, TILE), TILE), :]
            right = columns_ref[pl.ds(pl.multiple_of(j * TILE, TILE), TILE), :]
            product = lax.dot_general(left, right, (((1,), (1,)), ((), ())), preferred_element_type=jnp.float32)
            at = pl.multiple_of(owner * half + index * TILE, TILE)
            part[pl.ds(at, TILE), :] = product * scale

    other = (core + 1) % 2
    gram_blocks(other)
    pair = pltpu.make_async_remote_copy(
        src_ref=part.at[pl.ds(pl.multiple_of(other * half, half), half)], dst_ref=pair_land,
        send_sem=pair_send, recv_sem=pair_recv,
        device_id={"af": fiber_at(0, 1)}, device_id_type=MESH,
    )
    pair.start()
    gram_blocks(core)
    pair.wait()
    my_half = pl.ds(pl.multiple_of(core * half, half), half)
    pair_sum[...] = part[my_half, :] + pair_land[...]

    copies = []
    for step in ring_offsets(x_size):
        peer = (x + step) % x_size
        copy = pltpu.make_async_remote_copy(
            src_ref=pair_sum.at[pl.ds(pl.multiple_of(peer * x_rows, x_rows), x_rows)], dst_ref=x_land.at[step - 1],
            send_sem=x_send.at[step - 1], recv_sem=x_recv.at[step - 1],
            device_id={"gy": peer}, device_id_type=MESH,
        )
        copy.start()
        copies.append(copy)
    for copy in copies:
        copy.wait()
    total = pair_sum[pl.ds(pl.multiple_of(x * x_rows, x_rows), x_rows), :]
    for step in range(1, x_size):
        total = total + x_land[step - 1]
    x_sum[...] = total

    def tile_start(owner):
        return (owner * (x_rows // 8) // y_size) * 8

    copies = []
    for step in ring_offsets(y_size):
        peer = (y + step) % y_size
        copy = pltpu.make_async_remote_copy(
            src_ref=x_sum.at[pl.ds(pl.multiple_of(tile_start(peer), 8), y_rows)], dst_ref=y_land.at[step - 1],
            send_sem=y_send.at[step - 1], recv_sem=y_recv.at[step - 1],
            device_id={"gz": peer}, device_id_type=MESH,
        )
        copy.start()
        copies.append(copy)
    for copy in copies:
        copy.wait()
    total = x_sum[pl.ds(pl.multiple_of(tile_start(y), 8), y_rows), :]
    for step in range(1, y_size):
        total = total + y_land[step - 1]

    z_land[z] = total
    copies = []
    for step in ring_offsets(z_size):
        peer = fiber_at(step, 0)
        copy = pltpu.make_async_remote_copy(
            src_ref=z_land.at[z], dst_ref=z_land.at[z],
            send_sem=z_send.at[step - 1], recv_sem=z_recv.at[step - 1],
            device_id={"af": peer}, device_id_type=MESH,
        )
        copy.start()
        copies.append(copy)
    for copy in copies:
        copy.wait()
    total = z_land[0]
    for index in range(1, z_size):
        total = total + z_land[index]

    pieces_ref[core, x, 0] = total
    near = sorted(range(1, y_size), key=lambda step: min(step, y_size - step))
    sent = []

    def copy_of(src, dst, sems, index, target):
        return pltpu.make_async_remote_copy(
            src_ref=pieces_ref.at[src], dst_ref=pieces_ref.at[dst],
            send_sem=sems[0].at[index], recv_sem=sems[1].at[index],
            device_id=target, device_id_type=MESH,
        )

    def send(*args):
        copy = copy_of(*args)
        copy.start()
        sent.append(copy)

    y_sems, x_sems, pair_sems = (yg_send, yg_recv), (xg_send, xg_recv), (final_send, final_recv)
    partner = {"af": fiber_at(0, 1)}
    other = (core + 1) % 2
    for place in range(y_size - 1, 0, -1):
        target = {"gz": (y + near[place - 1]) % y_size}
        send((core, x, 0), (core, x, place), y_sems, place - 1, target)
    groups = [pl.ds(0, y_size // 2), pl.ds(y_size // 2, y_size // 2)]
    x_steps = sorted(range(1, x_size), key=lambda step: min(step, x_size - step))
    for number, group in enumerate(groups):
        for place in range(max(group.start, 1), group.start + group.size):
            target = {"gz": (y + near[place - 1]) % y_size}
            copy_of((core, x, 0), (core, x, place), y_sems, place - 1, target).wait_recv()
        mine = (core, x, group)
        for step in reversed(x_steps):
            send(mine, mine, x_sems, (step - 1) * 2 + number, {"gy": (x + step) % x_size})
        send(mine, mine, pair_sems, number, partner)
    for number, group in enumerate(groups):
        for step in x_steps:
            origin = (x + x_size - step) % x_size
            theirs = (core, origin, group)
            copy_of(theirs, theirs, x_sems, (step - 1) * 2 + number, {"gy": origin}).wait_recv()
            send(theirs, theirs, pair_sems, step * 2 + number, partner)
    for number, group in enumerate(groups):
        for step in range(x_size):
            theirs = (other, (x + x_size - step) % x_size, group)
            copy_of(theirs, theirs, pair_sems, step * 2 + number, partner).wait_recv()
    for copy in sent:
        copy.wait_send()


def arrange_kernel(owner_ref, slab_ref, out_ref, owners, slab, sems):
    fibers, _, block_cols = out_ref.shape
    loads = [
        pltpu.make_async_copy(owner_ref, owners, sems.at[0]),
        pltpu.make_async_copy(slab_ref, slab, sems.at[1]),
    ]
    for load in loads:
        load.start()
    loads[0].wait()
    starts = []
    for target in range(fibers):
        source = jnp.int32(0)
        for block in range(1, fibers):
            source = source + jnp.where(owners[0, 0, block] == target, block, 0)
        starts.append(pl.multiple_of(source * block_cols, block_cols))
    loads[1].wait()
    for target in range(fibers):
        out_ref[target] = slab[:, pl.ds(starts[target], block_cols)]


def arrange(owners, slab):
    fibers = owners.shape[-1]
    rows, width = slab.shape
    return pl.pallas_call(
        arrange_kernel,
        out_shape=jax.ShapeDtypeStruct((fibers, rows, width // fibers), slab.dtype),
        in_specs=[pl.BlockSpec(memory_space=pl.ANY)] * 2,
        out_specs=pl.BlockSpec(memory_space=pltpu.VMEM),
        scratch_shapes=[
            pltpu.SMEM(owners.shape, jnp.int32), pltpu.VMEM(slab.shape, slab.dtype), pltpu.SemaphoreType.DMA((2,)),
        ],
    )(owners, slab)


def exchange(arranged):
    sizes = (lax.axis_size("af"), lax.axis_size("gy"), lax.axis_size("gz"))
    fibers, x_size, y_size = sizes
    z_size = fibers // 2
    rows, block_cols = arranged.shape[1:]
    all_rows = rows * fibers
    half = 5 * TILE
    x_rows = half // x_size
    y_rows = max(
        (((p + 1) * (x_rows // 8)) // y_size - (p * (x_rows // 8)) // y_size) for p in range(y_size)
    ) * 8
    dma = pltpu.SemaphoreType.DMA
    f32, bf16 = jnp.float32, jnp.bfloat16
    return pl.pallas_call(
        functools.partial(exchange_kernel, sizes),
        out_shape=(
            jax.ShapeDtypeStruct((all_rows, block_cols), bf16),
            jax.ShapeDtypeStruct((2, x_size, y_size, y_rows, TILE), f32),
        ),
        in_specs=[pl.BlockSpec(memory_space=pltpu.VMEM)],
        out_specs=[pl.BlockSpec(memory_space=pltpu.VMEM)] * 2,
        scratch_shapes=[
            pltpu.VMEM((2 * half, TILE), f32),
            pltpu.VMEM((half, TILE), f32),
            pltpu.VMEM((half, TILE), f32),
            pltpu.VMEM((x_size - 1, x_rows, TILE), f32),
            pltpu.VMEM((x_rows, TILE), f32),
            pltpu.VMEM((y_size - 1, y_rows, TILE), f32),
            pltpu.VMEM((z_size, y_rows, TILE), f32),
            dma((fibers - 1,)), dma((fibers - 1,)), dma, dma,
            dma((x_size - 1,)), dma((x_size - 1,)), dma((y_size - 1,)), dma((y_size - 1,)),
            dma((z_size - 1,)), dma((z_size - 1,)),
            dma((y_size - 1,)), dma((y_size - 1,)),
            dma(((x_size - 1) * 2,)), dma(((x_size - 1) * 2,)),
            dma((x_size * 2,)), dma((x_size * 2,)),
        ],
        compiler_params=pltpu.CompilerParams(collective_id=0, has_side_effects=True, vmem_limit_bytes=32 << 20),
    )(arranged)


NN, NT, TN = ((1,), (0,)), ((1,), (1,)), ((0,), (0,))


def parts_of(a):
    f32, bf16 = jnp.float32, jnp.bfloat16
    high = a.astype(bf16).astype(f32)
    rest = a - high
    middle = rest.astype(bf16).astype(f32)
    return high, middle, rest - middle


def stacked(a, order, axis):
    parts = parts_of(a)
    return jnp.concatenate([parts[k] for k in order], axis=axis).astype(jnp.bfloat16)


LEFT, RIGHT = (0, 0, 1, 1, 0, 2), (0, 1, 0, 1, 2, 0)
MID = 4


def dot_exact(a, b, dims, terms=6):
    (da,), (db,) = dims
    return lax.dot_general(
        stacked(a, LEFT[:terms], da), stacked(b, RIGHT[:terms], db), (dims, ((), ())), preferred_element_type=jnp.float32
    )


def eliminate_strip(work, final, scales, first):
    f32 = jnp.float32
    shape = (STRIP, TILE)
    lane = lax.broadcasted_iota(jnp.int32, shape, 1)
    sub = lax.broadcasted_iota(jnp.int32, shape, 0)
    strip = work[pl.ds(first, STRIP), :]
    heads = [
        jnp.take_along_axis(strip, jnp.full(shape, first + t, jnp.int32), axis=1) for t in range(STRIP)
    ]
    full = strip
    down = strip
    scale = jnp.zeros(shape, f32)
    for t in range(STRIP):
        head = heads[t]
        pivot = jnp.broadcast_to(head[t : t + 1, :], shape)
        inverse = 1.0 / pivot
        scale = jnp.where(sub == t, lax.rsqrt(pivot), scale)
        factor = head * inverse
        here = lane == first + t
        row = jnp.where(here, 1.0, jnp.broadcast_to(full[t : t + 1, :], shape))
        full = jnp.where(sub == t, row * inverse, jnp.where(here, 0.0, full) - factor * row)
        drow = jnp.where(here, 1.0, jnp.broadcast_to(down[t : t + 1, :], shape))
        down = jnp.where(sub > t, jnp.where(here, 0.0, down) - factor * drow, down)
        for u in range(t + 1, STRIP):
            line = jnp.broadcast_to(heads[u][t : t + 1, :], shape)
            heads[u] = jnp.where(sub == t, line * inverse, heads[u] - factor * line)
    final[pl.ds(first, STRIP), :] = down * scale
    scales[pl.ds(first, STRIP), :] = scale
    later = jnp.where(lane >= first + STRIP, strip, 0.0)
    return full, later


def strip_update(work, full, later, first):
    lane = lax.broadcasted_iota(jnp.int32, (TILE, TILE), 1)
    own = (lane >= first) & (lane < first + STRIP)
    update = dot_exact(later, full, TN)
    work[...] = jnp.where(own, 0.0, work[...]) - update


def factor_both(works, finals, scales):
    @pl.loop(0, TILE // STRIP)
    def _(index):
        first = pl.multiple_of(index * STRIP, STRIP)
        pieces = [eliminate_strip(w, f, s, first) for w, f, s in zip(works, finals, scales)]
        for work, (full, later) in zip(works, pieces):
            strip_update(work, full, later, first)


def inverse_of(final, scales):
    lane = lax.broadcasted_iota(jnp.int32, (TILE, TILE), 1)
    sub = lax.broadcasted_iota(jnp.int32, (TILE, TILE), 0)
    return jnp.where(lane < sub, final[...], jnp.where(lane == sub, scales[...], 0.0))


def upper_of(final):
    lane = lax.broadcasted_iota(jnp.int32, (TILE, TILE), 1)
    sub = lax.broadcasted_iota(jnp.int32, (TILE, TILE), 0)
    return jnp.where(lane >= sub, final[...], 0.0)


def factor_kernel(
    pieces_ref, start_ref, columns_ref, triangle_ref, basis_ref, core_ref,
    packed_ref, gram, trail, product, work_a, work_b, final_a, final_b, scale_a, scale_b,
):
    count = 4
    cores, x_size, y_size, _, _ = pieces_ref.shape
    tiles = packed_ref.shape[0] // 8 // cores // x_size
    here = lax.axis_index("gz")
    for y in range(y_size):
        step = (here + y_size - y) % y_size
        near = jnp.minimum(step, y_size - step)
        place = 2 * near - jnp.where((step > 0) & (step <= y_size // 2), 1, 0)
        for c in range(cores):
            for x in range(x_size):
                first, last = tiles * y // y_size, tiles * (y + 1) // y_size
                spread = pl.ds(((c * x_size + x) * tiles + first) * 8, (last - first) * 8)
                packed_ref[spread, :] = pieces_ref[c, x, place, : (last - first) * 8, :]
    spot = lambda i, j: pl.ds((i * (i + 1) // 2 + j) * TILE, TILE)
    at = lambda i: pl.ds(i * TILE, TILE)
    for i in range(count):
        for j in range(i + 1):
            block = packed_ref[spot(i, j), :]
            gram[at(i), at(j)] = block
            trail[at(i), at(j)] = block
            if i != j:
                gram[at(j), at(i)] = block.T
                triangle_ref[at(j), at(i)] = jnp.zeros((TILE, TILE), jnp.float32)
    start = start_ref[...]
    image = dot_exact(gram[...], start, NN, MID)
    product[...] = image
    work_b[...] = dot_exact(start, image, TN, MID)
    for k in range(count):
        work_a[...] = trail[at(k), at(k)]
        factor_both((work_a, work_b), (final_a, final_b), (scale_a, scale_b))
        turn = inverse_of(final_b, scale_b)
        image = dot_exact(product[...], turn, NT, 6 if k == count - 1 else MID)
        if k == 0 or k == 2:
            product[...] = image
            work_b[...] = dot_exact(image, image, TN, 6 if k == 2 else MID)
        elif k == 1:
            moved = dot_exact(gram[...], image, NN, MID)
            product[...] = moved
            work_b[...] = dot_exact(image, moved, TN, MID)
        else:
            basis_ref[...] = image
            core_ref[...] = lax.dot_general(
                image.astype(jnp.bfloat16), columns_ref[...], (TN, ((), ())), preferred_element_type=jnp.float32
            ).astype(jnp.bfloat16)
        triangle_ref[at(k), at(k)] = upper_of(final_a).T
        if k + 1 < count:
            rest = pl.ds((k + 1) * TILE, (count - 1 - k) * TILE)
            lower = dot_exact(trail[rest, at(k)], inverse_of(final_a, scale_a), NT)
            triangle_ref[rest, at(k)] = lower
            for j in range(k + 1, count):
                tail = pl.ds(j * TILE, (count - j) * TILE)
                skip = (j - k - 1) * TILE
                trail[tail, at(j)] = trail[tail, at(j)] - dot_exact(lower[skip:], lower[skip : skip + TILE], NT)


def factor(pieces, start, columns):
    f32 = jnp.float32
    rows, rank = start.shape
    square = pltpu.VMEM((TILE, TILE), f32)
    return pl.pallas_call(
        factor_kernel,
        out_shape=(
            jax.ShapeDtypeStruct((rows, rows), f32),
            jax.ShapeDtypeStruct((rows, rank), f32),
            jax.ShapeDtypeStruct((rank, columns.shape[1]), jnp.bfloat16),
        ),
        in_specs=[pl.BlockSpec(memory_space=pltpu.VMEM)] * 3,
        out_specs=[pl.BlockSpec(memory_space=pltpu.VMEM)] * 3,
        scratch_shapes=[
            pltpu.VMEM((10 * TILE, TILE), f32), pltpu.VMEM((rows, rows), f32), pltpu.VMEM((rows, rows), f32), pltpu.VMEM((rows, rank), f32),
            square, square, square, square, square, square,
        ],
        compiler_params=pltpu.CompilerParams(vmem_limit_bytes=32 << 20),
    )(pieces, start, columns)


def on_device(slab, block_owner, basis_init):
    columns, packed = exchange(arrange(block_owner, slab))
    return factor(packed, basis_init, columns)


def solution(mesh):
    placed = (P("af", ("gy", "gz")), P("gy", "gz", None), P())
    return jax.shard_map(
        on_device,
        mesh=mesh,
        in_specs=placed,
        out_specs=(P(), P(), P(None, ("gy", "gz", "af"))),
        check_vma=False,
    )
```

```python
import functools
import jax
import jax.numpy as jnp
from jax import lax
from jax.experimental import pallas as pl
from jax.experimental.pallas import tpu as pltpu
from jax.sharding import PartitionSpec as P

TILE = 128
STRIP = 8
exact_mode = lax.Precision.HIGHEST
MESH = pl.DeviceIdType.MESH


def ring_offsets(size):
    return sorted(range(1, size), key=lambda step: -min(step, size - step))


def exchange_kernel(
    sizes, outgoing, columns_ref, pieces_ref,
    part, pair_land, pair_sum, x_land, x_sum, y_land, z_land,
    a2a_send, a2a_recv, pair_send, pair_recv, x_send, x_recv, y_send, y_recv, z_send, z_recv,
    yg_send, yg_recv, xg_send, xg_recv, final_send, final_recv,
):
    fibers, x_size, y_size = sizes
    z_size = fibers // 2
    rows, block_cols = outgoing.shape[1:]
    fiber = lax.axis_index("af")
    x = lax.axis_index("gy")
    y = lax.axis_index("gz")
    z, core = fiber // 2, fiber % 2
    half = pair_sum.shape[0]
    x_rows = x_sum.shape[0]
    y_rows = y_land.shape[1]

    def fiber_at(z_step, core_step):
        return ((z + z_step) % z_size) * 2 + (core + core_step) % 2

    fiber_steps = [(0, 1)] + [(s, c) for s in reversed(ring_offsets(z_size)) for c in (0, 1)]
    barrier = pltpu.get_barrier_semaphore()
    for z_step, core_step in fiber_steps:
        pl.semaphore_signal(barrier, inc=1, device_id={"af": fiber_at(z_step, core_step)}, device_id_type=MESH)
    for step in range(1, y_size):
        pl.semaphore_signal(barrier, inc=1, device_id={"gz": (y + step) % y_size}, device_id_type=MESH)
    for step in range(1, x_size):
        pl.semaphore_signal(barrier, inc=1, device_id={"gy": (x + step) % x_size}, device_id_type=MESH)

    pl.semaphore_wait(barrier, len(fiber_steps) + x_size + y_size - 2)

    my_rows = pl.ds(pl.multiple_of(fiber * rows, rows), rows)
    copies = []
    for index, (z_step, core_step) in enumerate(fiber_steps):
        peer = fiber_at(z_step, core_step)
        copy = pltpu.make_async_remote_copy(
            src_ref=outgoing.at[peer], dst_ref=columns_ref.at[my_rows],
            send_sem=a2a_send.at[index], recv_sem=a2a_recv.at[index],
            device_id={"af": peer}, device_id_type=MESH,
        )
        copy.start()
        copies.append(copy)
    columns_ref[my_rows, :] = outgoing[fiber]
    for copy in copies:
        copy.wait()

    scale = 1.0 / (block_cols * fibers * x_size * y_size)
    pairs = [(i, j) for i in range(4) for j in range(i + 1)]
    per_core = len(pairs) // 2

    def gram_blocks(owner):
        for index in range(per_core):
            (i0, j0), (i1, j1) = pairs[index], pairs[per_core + index]
            i = i0 + owner * (i1 - i0)
            j = j0 + owner * (j1 - j0)
            left = columns_ref[pl.ds(pl.multiple_of(i * TILE, TILE), TILE), :]
            right = columns_ref[pl.ds(pl.multiple_of(j * TILE, TILE), TILE), :]
            product = lax.dot_general(left, right, (((1,), (1,)), ((), ())), preferred_element_type=jnp.float32)
            at = pl.multiple_of(owner * half + index * TILE, TILE)
            part[pl.ds(at, TILE), :] = product * scale

    other = (core + 1) % 2
    gram_blocks(other)
    pair = pltpu.make_async_remote_copy(
        src_ref=part.at[pl.ds(pl.multiple_of(other * half, half), half)], dst_ref=pair_land,
        send_sem=pair_send, recv_sem=pair_recv,
        device_id={"af": fiber_at(0, 1)}, device_id_type=MESH,
    )
    pair.start()
    gram_blocks(core)
    pair.wait()
    my_half = pl.ds(pl.multiple_of(core * half, half), half)
    pair_sum[...] = part[my_half, :] + pair_land[...]

    copies = []
    for step in ring_offsets(x_size):
        peer = (x + step) % x_size
        copy = pltpu.make_async_remote_copy(
            src_ref=pair_sum.at[pl.ds(pl.multiple_of(peer * x_rows, x_rows), x_rows)], dst_ref=x_land.at[step - 1],
            send_sem=x_send.at[step - 1], recv_sem=x_recv.at[step - 1],
            device_id={"gy": peer}, device_id_type=MESH,
        )
        copy.start()
        copies.append(copy)
    for copy in copies:
        copy.wait()
    total = pair_sum[pl.ds(pl.multiple_of(x * x_rows, x_rows), x_rows), :]
    for step in range(1, x_size):
        total = total + x_land[step - 1]
    x_sum[...] = total

    def tile_start(owner):
        return (owner * (x_rows // 8) // y_size) * 8

    copies = []
    for step in ring_offsets(y_size):
        peer = (y + step) % y_size
        copy = pltpu.make_async_remote_copy(
            src_ref=x_sum.at[pl.ds(pl.multiple_of(tile_start(peer), 8), y_rows)], dst_ref=y_land.at[step - 1],
            send_sem=y_send.at[step - 1], recv_sem=y_recv.at[step - 1],
            device_id={"gz": peer}, device_id_type=MESH,
        )
        copy.start()
        copies.append(copy)
    for copy in copies:
        copy.wait()
    total = x_sum[pl.ds(pl.multiple_of(tile_start(y), 8), y_rows), :]
    for step in range(1, y_size):
        total = total + y_land[step - 1]

    z_land[z] = total
    copies = []
    for step in ring_offsets(z_size):
        peer = fiber_at(step, 0)
        copy = pltpu.make_async_remote_copy(
            src_ref=z_land.at[z], dst_ref=z_land.at[z],
            send_sem=z_send.at[step - 1], recv_sem=z_recv.at[step - 1],
            device_id={"af": peer}, device_id_type=MESH,
        )
        copy.start()
        copies.append(copy)
    for copy in copies:
        copy.wait()
    total = z_land[0]
    for index in range(1, z_size):
        total = total + z_land[index]

    pieces_ref[core, x, 0] = total
    near = sorted(range(1, y_size), key=lambda step: min(step, y_size - step))
    sent = []

    def copy_of(src, dst, sems, index, target):
        return pltpu.make_async_remote_copy(
            src_ref=pieces_ref.at[src], dst_ref=pieces_ref.at[dst],
            send_sem=sems[0].at[index], recv_sem=sems[1].at[index],
            device_id=target, device_id_type=MESH,
        )

    def send(*args):
        copy = copy_of(*args)
        copy.start()
        sent.append(copy)

    y_sems, x_sems, pair_sems = (yg_send, yg_recv), (xg_send, xg_recv), (final_send, final_recv)
    partner = {"af": fiber_at(0, 1)}
    other = (core + 1) % 2
    for place in range(y_size - 1, 0, -1):
        target = {"gz": (y + near[place - 1]) % y_size}
        send((core, x, 0), (core, x, place), y_sems, place - 1, target)
    groups = [pl.ds(0, y_size // 2), pl.ds(y_size // 2, y_size // 2)]
    x_steps = sorted(range(1, x_size), key=lambda step: min(step, x_size - step))
    for number, group in enumerate(groups):
        for place in range(max(group.start, 1), group.start + group.size):
            target = {"gz": (y + near[place - 1]) % y_size}
            copy_of((core, x, 0), (core, x, place), y_sems, place - 1, target).wait_recv()
        mine = (core, x, group)
        for step in reversed(x_steps):
            send(mine, mine, x_sems, (step - 1) * 2 + number, {"gy": (x + step) % x_size})
        send(mine, mine, pair_sems, number, partner)
    for number, group in enumerate(groups):
        for step in x_steps:
            origin = (x + x_size - step) % x_size
            theirs = (core, origin, group)
            copy_of(theirs, theirs, x_sems, (step - 1) * 2 + number, {"gy": origin}).wait_recv()
            send(theirs, theirs, pair_sems, step * 2 + number, partner)
    for number, group in enumerate(groups):
        for step in range(x_size):
            theirs = (other, (x + x_size - step) % x_size, group)
            copy_of(theirs, theirs, pair_sems, step * 2 + number, partner).wait_recv()
    for copy in sent:
        copy.wait_send()


def arrange_kernel(owner_ref, slab_ref, out_ref, owners, slab, sems):
    fibers, _, block_cols = out_ref.shape
    loads = [
        pltpu.make_async_copy(owner_ref, owners, sems.at[0]),
        pltpu.make_async_copy(slab_ref, slab, sems.at[1]),
    ]
    for load in loads:
        load.start()
    loads[0].wait()
    starts = []
    for target in range(fibers):
        source = jnp.int32(0)
        for block in range(1, fibers):
            source = source + jnp.where(owners[0, 0, block] == target, block, 0)
        starts.append(pl.multiple_of(source * block_cols, block_cols))
    loads[1].wait()
    for target in range(fibers):
        out_ref[target] = slab[:, pl.ds(starts[target], block_cols)]


def arrange(owners, slab):
    fibers = owners.shape[-1]
    rows, width = slab.shape
    return pl.pallas_call(
        arrange_kernel,
        out_shape=jax.ShapeDtypeStruct((fibers, rows, width // fibers), slab.dtype),
        in_specs=[pl.BlockSpec(memory_space=pl.ANY)] * 2,
        out_specs=pl.BlockSpec(memory_space=pltpu.VMEM),
        scratch_shapes=[
            pltpu.SMEM(owners.shape, jnp.int32), pltpu.VMEM(slab.shape, slab.dtype), pltpu.SemaphoreType.DMA((2,)),
        ],
    )(owners, slab)


def exchange(arranged):
    sizes = (lax.axis_size("af"), lax.axis_size("gy"), lax.axis_size("gz"))
    fibers, x_size, y_size = sizes
    z_size = fibers // 2
    rows, block_cols = arranged.shape[1:]
    all_rows = rows * fibers
    half = 5 * TILE
    x_rows = half // x_size
    y_rows = max(
        (((p + 1) * (x_rows // 8)) // y_size - (p * (x_rows // 8)) // y_size) for p in range(y_size)
    ) * 8
    dma = pltpu.SemaphoreType.DMA
    f32, bf16 = jnp.float32, jnp.bfloat16
    return pl.pallas_call(
        functools.partial(exchange_kernel, sizes),
        out_shape=(
            jax.ShapeDtypeStruct((all_rows, block_cols), bf16),
            jax.ShapeDtypeStruct((2, x_size, y_size, y_rows, TILE), f32),
        ),
        in_specs=[pl.BlockSpec(memory_space=pltpu.VMEM)],
        out_specs=[pl.BlockSpec(memory_space=pltpu.VMEM)] * 2,
        scratch_shapes=[
            pltpu.VMEM((2 * half, TILE), f32),
            pltpu.VMEM((half, TILE), f32),
            pltpu.VMEM((half, TILE), f32),
            pltpu.VMEM((x_size - 1, x_rows, TILE), f32),
            pltpu.VMEM((x_rows, TILE), f32),
            pltpu.VMEM((y_size - 1, y_rows, TILE), f32),
            pltpu.VMEM((z_size, y_rows, TILE), f32),
            dma((fibers - 1,)), dma((fibers - 1,)), dma, dma,
            dma((x_size - 1,)), dma((x_size - 1,)), dma((y_size - 1,)), dma((y_size - 1,)),
            dma((z_size - 1,)), dma((z_size - 1,)),
            dma((y_size - 1,)), dma((y_size - 1,)),
            dma(((x_size - 1) * 2,)), dma(((x_size - 1) * 2,)),
            dma((x_size * 2,)), dma((x_size * 2,)),
        ],
        compiler_params=pltpu.CompilerParams(collective_id=0, has_side_effects=True, vmem_limit_bytes=32 << 20),
    )(arranged)


NN, NT, TN = ((1,), (0,)), ((1,), (1,)), ((0,), (0,))


def parts_of(a):
    f32, bf16 = jnp.float32, jnp.bfloat16
    high = a.astype(bf16).astype(f32)
    rest = a - high
    middle = rest.astype(bf16).astype(f32)
    return high, middle, rest - middle


def stacked(a, order, axis):
    parts = parts_of(a)
    return jnp.concatenate([parts[k] for k in order], axis=axis).astype(jnp.bfloat16)


LEFT, RIGHT = (0, 0, 1, 1, 0, 2), (0, 1, 0, 1, 2, 0)
MID = 4


def dot_exact(a, b, dims, terms=6):
    (da,), (db,) = dims
    return lax.dot_general(
        stacked(a, LEFT[:terms], da), stacked(b, RIGHT[:terms], db), (dims, ((), ())), preferred_element_type=jnp.float32
    )


def eliminate_strip(strip, final, scales, first):
    f32 = jnp.float32
    shape = (STRIP, TILE)
    lane = lax.broadcasted_iota(jnp.int32, shape, 1)
    sub = lax.broadcasted_iota(jnp.int32, shape, 0)
    heads = [
        jnp.take_along_axis(strip, jnp.full(shape, first + t, jnp.int32), axis=1) for t in range(STRIP)
    ]
    full = strip
    down = strip
    scale = jnp.zeros(shape, f32)
    for t in range(STRIP):
        head = heads[t]
        pivot = jnp.broadcast_to(head[t : t + 1, :], shape)
        inverse = 1.0 / pivot
        scale = jnp.where(sub == t, lax.rsqrt(pivot), scale)
        factor = head * inverse
        here = lane == first + t
        row = jnp.where(here, 1.0, jnp.broadcast_to(full[t : t + 1, :], shape))
        full = jnp.where(sub == t, row * inverse, jnp.where(here, 0.0, full) - factor * row)
        drow = jnp.where(here, 1.0, jnp.broadcast_to(down[t : t + 1, :], shape))
        down = jnp.where(sub > t, jnp.where(here, 0.0, down) - factor * drow, down)
        for u in range(t + 1, STRIP):
            line = jnp.broadcast_to(heads[u][t : t + 1, :], shape)
            heads[u] = jnp.where(sub == t, line * inverse, heads[u] - factor * line)
    final[pl.ds(first, STRIP), :] = down * scale
    scales[pl.ds(first, STRIP), :] = scale
    return full


def stacked_wide(a, order):
    parts = parts_of(a)
    return jnp.concatenate([parts[k] for k in order], axis=0)


def advance(strip, full, work, left, right, first):
    shape = (STRIP, TILE)
    lane = lax.broadcasted_iota(jnp.int32, shape, 1)
    later = jnp.where(lane >= first + STRIP, strip, 0.0)
    left[...] = stacked_wide(later, LEFT).astype(jnp.bfloat16).T
    right[...] = stacked_wide(full, RIGHT).astype(jnp.bfloat16)
    onward = pl.ds(pl.multiple_of(jnp.minimum(first + STRIP, TILE - STRIP), STRIP), STRIP)
    own = (lane >= first) & (lane < first + STRIP)
    following = jnp.where(own, 0.0, work[onward, :])
    sub = lax.broadcasted_iota(jnp.int32, shape, 0)
    change = jnp.zeros(shape, jnp.float32)
    for s in range(STRIP):
        spot = jnp.full(shape, jnp.minimum(first + STRIP + s, TILE - 1), jnp.int32)
        line = jnp.sum(jnp.take_along_axis(strip, spot, axis=1) * full, axis=0, keepdims=True)
        change = jnp.where(sub == s, jnp.broadcast_to(line, shape), change)
    return following - change


def apply_update(work, left, right, first):
    lane = lax.broadcasted_iota(jnp.int32, (TILE, TILE), 1)
    before = (lane >= first - STRIP) & (lane < first)
    update = jnp.dot(left[...], right[...], preferred_element_type=jnp.float32)
    work[...] = jnp.where(before, 0.0, work[...]) - update


def factor_both(works, finals, scales, lefts, rights):
    for left, right in zip(lefts, rights):
        left[...] = jnp.zeros_like(left)
        right[...] = jnp.zeros_like(right)

    def step(index, strips):
        first = pl.multiple_of(index * STRIP, STRIP)
        for work, left, right in zip(works, lefts, rights):
            apply_update(work, left, right, first)
        fulls = [eliminate_strip(v, f, s, first) for v, f, s in zip(strips, finals, scales)]
        return tuple(
            advance(*group, first) for group in zip(strips, fulls, works, lefts, rights)
        )

    lax.fori_loop(0, TILE // STRIP, step, tuple(work[:STRIP, :] for work in works))


def inverse_of(final, scales):
    lane = lax.broadcasted_iota(jnp.int32, (TILE, TILE), 1)
    sub = lax.broadcasted_iota(jnp.int32, (TILE, TILE), 0)
    return jnp.where(lane < sub, final[...], jnp.where(lane == sub, scales[...], 0.0))


def upper_of(final):
    lane = lax.broadcasted_iota(jnp.int32, (TILE, TILE), 1)
    sub = lax.broadcasted_iota(jnp.int32, (TILE, TILE), 0)
    return jnp.where(lane >= sub, final[...], 0.0)


def factor_kernel(
    pieces_ref, start_ref, columns_ref, triangle_ref, basis_ref, core_ref,
    packed_ref, gram, trail, product, work_a, work_b, final_a, final_b, scale_a, scale_b,
    left_a, left_b, right_a, right_b,
):
    count = 4
    cores, x_size, y_size, _, _ = pieces_ref.shape
    tiles = packed_ref.shape[0] // 8 // cores // x_size
    here = lax.axis_index("gz")
    for y in range(y_size):
        step = (here + y_size - y) % y_size
        near = jnp.minimum(step, y_size - step)
        place = 2 * near - jnp.where((step > 0) & (step <= y_size // 2), 1, 0)
        for c in range(cores):
            for x in range(x_size):
                first, last = tiles * y // y_size, tiles * (y + 1) // y_size
                spread = pl.ds(((c * x_size + x) * tiles + first) * 8, (last - first) * 8)
                packed_ref[spread, :] = pieces_ref[c, x, place, : (last - first) * 8, :]
    spot = lambda i, j: pl.ds((i * (i + 1) // 2 + j) * TILE, TILE)
    at = lambda i: pl.ds(i * TILE, TILE)
    for i in range(count):
        for j in range(i + 1):
            block = packed_ref[spot(i, j), :]
            gram[at(i), at(j)] = block
            trail[at(i), at(j)] = block
            if i != j:
                gram[at(j), at(i)] = block.T
                triangle_ref[at(j), at(i)] = jnp.zeros((TILE, TILE), jnp.float32)
    start = start_ref[...]
    image = dot_exact(gram[...], start, NN, MID)
    product[...] = image
    work_b[...] = dot_exact(start, image, TN, MID)
    for k in range(count):
        work_a[...] = trail[at(k), at(k)]
        factor_both(
            (work_a, work_b), (final_a, final_b), (scale_a, scale_b),
            (left_a, left_b), (right_a, right_b),
        )
        turn = inverse_of(final_b, scale_b)
        image = dot_exact(product[...], turn, NT, 6 if k == count - 1 else MID)
        if k == 0 or k == 2:
            product[...] = image
            work_b[...] = dot_exact(image, image, TN, 6 if k == 2 else MID)
        elif k == 1:
            moved = dot_exact(gram[...], image, NN, MID)
            product[...] = moved
            work_b[...] = dot_exact(image, moved, TN, MID)
        else:
            basis_ref[...] = image
            core_ref[...] = lax.dot_general(
                image.astype(jnp.bfloat16), columns_ref[...], (TN, ((), ())), preferred_element_type=jnp.float32
            ).astype(jnp.bfloat16)
        triangle_ref[at(k), at(k)] = upper_of(final_a).T
        if k + 1 < count:
            rest = pl.ds((k + 1) * TILE, (count - 1 - k) * TILE)
            lower = dot_exact(trail[rest, at(k)], inverse_of(final_a, scale_a), NT)
            triangle_ref[rest, at(k)] = lower
            for j in range(k + 1, count):
                tail = pl.ds(j * TILE, (count - j) * TILE)
                skip = (j - k - 1) * TILE
                trail[tail, at(j)] = trail[tail, at(j)] - dot_exact(lower[skip:], lower[skip : skip + TILE], NT)


def factor(pieces, start, columns):
    f32 = jnp.float32
    rows, rank = start.shape
    square = pltpu.VMEM((TILE, TILE), f32)
    wide, tall = pltpu.VMEM((TILE, 6 * STRIP), jnp.bfloat16), pltpu.VMEM((6 * STRIP, TILE), jnp.bfloat16)
    return pl.pallas_call(
        factor_kernel,
        out_shape=(
            jax.ShapeDtypeStruct((rows, rows), f32),
            jax.ShapeDtypeStruct((rows, rank), f32),
            jax.ShapeDtypeStruct((rank, columns.shape[1]), jnp.bfloat16),
        ),
        in_specs=[pl.BlockSpec(memory_space=pltpu.VMEM)] * 3,
        out_specs=[pl.BlockSpec(memory_space=pltpu.VMEM)] * 3,
        scratch_shapes=[
            pltpu.VMEM((10 * TILE, TILE), f32), pltpu.VMEM((rows, rows), f32), pltpu.VMEM((rows, rows), f32), pltpu.VMEM((rows, rank), f32),
            square, square, square, square, square, square,
            wide, wide, tall, tall,
        ],
        compiler_params=pltpu.CompilerParams(vmem_limit_bytes=32 << 20),
    )(pieces, start, columns)


def on_device(slab, block_owner, basis_init):
    columns, packed = exchange(arrange(block_owner, slab))
    return factor(packed, basis_init, columns)


def solution(mesh):
    placed = (P("af", ("gy", "gz")), P("gy", "gz", None), P())
    return jax.shard_map(
        on_device,
        mesh=mesh,
        in_specs=placed,
        out_specs=(P(), P(), P(None, ("gy", "gz", "af"))),
        check_vma=False,
    )
```

```python
import functools
import jax
import jax.numpy as jnp
from jax import lax
from jax.experimental import pallas as pl
from jax.experimental.pallas import tpu as pltpu
from jax.sharding import PartitionSpec as P

TILE = 128
STRIP = 8
exact_mode = lax.Precision.HIGHEST
MESH = pl.DeviceIdType.MESH


def ring_offsets(size):
    return sorted(range(1, size), key=lambda step: -min(step, size - step))


def exchange_kernel(
    sizes, outgoing, columns_ref, pieces_ref,
    part, pair_land, pair_sum, x_land, x_sum, y_land, z_land,
    a2a_send, a2a_recv, pair_send, pair_recv, x_send, x_recv, y_send, y_recv, z_send, z_recv,
    yg_send, yg_recv, xg_send, xg_recv, final_send, final_recv,
):
    fibers, x_size, y_size = sizes
    z_size = fibers // 2
    rows, block_cols = outgoing.shape[1:]
    fiber = lax.axis_index("af")
    x = lax.axis_index("gy")
    y = lax.axis_index("gz")
    z, core = fiber // 2, fiber % 2
    half = pair_sum.shape[0]
    x_rows = x_sum.shape[0]
    y_rows = y_land.shape[1]

    def fiber_at(z_step, core_step):
        return ((z + z_step) % z_size) * 2 + (core + core_step) % 2

    fiber_steps = [(0, 1)] + [(s, c) for s in reversed(ring_offsets(z_size)) for c in (0, 1)]
    barrier = pltpu.get_barrier_semaphore()
    for z_step, core_step in fiber_steps:
        pl.semaphore_signal(barrier, inc=1, device_id={"af": fiber_at(z_step, core_step)}, device_id_type=MESH)
    for step in range(1, y_size):
        pl.semaphore_signal(barrier, inc=1, device_id={"gz": (y + step) % y_size}, device_id_type=MESH)
    for step in range(1, x_size):
        pl.semaphore_signal(barrier, inc=1, device_id={"gy": (x + step) % x_size}, device_id_type=MESH)

    pl.semaphore_wait(barrier, len(fiber_steps) + x_size + y_size - 2)

    my_rows = pl.ds(pl.multiple_of(fiber * rows, rows), rows)
    copies = []
    for index, (z_step, core_step) in enumerate(fiber_steps):
        peer = fiber_at(z_step, core_step)
        copy = pltpu.make_async_remote_copy(
            src_ref=outgoing.at[peer], dst_ref=columns_ref.at[my_rows],
            send_sem=a2a_send.at[index], recv_sem=a2a_recv.at[index],
            device_id={"af": peer}, device_id_type=MESH,
        )
        copy.start()
        copies.append(copy)
    columns_ref[my_rows, :] = outgoing[fiber]
    for copy in copies:
        copy.wait()

    scale = 1.0 / (block_cols * fibers * x_size * y_size)
    pairs = [(i, j) for i in range(4) for j in range(i + 1)]
    per_core = len(pairs) // 2

    def gram_blocks(owner):
        for index in range(per_core):
            (i0, j0), (i1, j1) = pairs[index], pairs[per_core + index]
            i = i0 + owner * (i1 - i0)
            j = j0 + owner * (j1 - j0)
            left = columns_ref[pl.ds(pl.multiple_of(i * TILE, TILE), TILE), :]
            right = columns_ref[pl.ds(pl.multiple_of(j * TILE, TILE), TILE), :]
            product = lax.dot_general(left, right, (((1,), (1,)), ((), ())), preferred_element_type=jnp.float32)
            at = pl.multiple_of(owner * half + index * TILE, TILE)
            part[pl.ds(at, TILE), :] = product * scale

    other = (core + 1) % 2
    gram_blocks(other)
    pair = pltpu.make_async_remote_copy(
        src_ref=part.at[pl.ds(pl.multiple_of(other * half, half), half)], dst_ref=pair_land,
        send_sem=pair_send, recv_sem=pair_recv,
        device_id={"af": fiber_at(0, 1)}, device_id_type=MESH,
    )
    pair.start()
    gram_blocks(core)
    pair.wait()
    my_half = pl.ds(pl.multiple_of(core * half, half), half)
    pair_sum[...] = part[my_half, :] + pair_land[...]

    copies = []
    for step in ring_offsets(x_size):
        peer = (x + step) % x_size
        copy = pltpu.make_async_remote_copy(
            src_ref=pair_sum.at[pl.ds(pl.multiple_of(peer * x_rows, x_rows), x_rows)], dst_ref=x_land.at[step - 1],
            send_sem=x_send.at[step - 1], recv_sem=x_recv.at[step - 1],
            device_id={"gy": peer}, device_id_type=MESH,
        )
        copy.start()
        copies.append(copy)
    for copy in copies:
        copy.wait()
    total = pair_sum[pl.ds(pl.multiple_of(x * x_rows, x_rows), x_rows), :]
    for step in range(1, x_size):
        total = total + x_land[step - 1]
    x_sum[...] = total

    def tile_start(owner):
        return (owner * (x_rows // 8) // y_size) * 8

    copies = []
    for step in ring_offsets(y_size):
        peer = (y + step) % y_size
        copy = pltpu.make_async_remote_copy(
            src_ref=x_sum.at[pl.ds(pl.multiple_of(tile_start(peer), 8), y_rows)], dst_ref=y_land.at[step - 1],
            send_sem=y_send.at[step - 1], recv_sem=y_recv.at[step - 1],
            device_id={"gz": peer}, device_id_type=MESH,
        )
        copy.start()
        copies.append(copy)
    for copy in copies:
        copy.wait()
    total = x_sum[pl.ds(pl.multiple_of(tile_start(y), 8), y_rows), :]
    for step in range(1, y_size):
        total = total + y_land[step - 1]

    z_land[z] = total
    copies = []
    for step in ring_offsets(z_size):
        peer = fiber_at(step, 0)
        copy = pltpu.make_async_remote_copy(
            src_ref=z_land.at[z], dst_ref=z_land.at[z],
            send_sem=z_send.at[step - 1], recv_sem=z_recv.at[step - 1],
            device_id={"af": peer}, device_id_type=MESH,
        )
        copy.start()
        copies.append(copy)
    for copy in copies:
        copy.wait()
    total = z_land[0]
    for index in range(1, z_size):
        total = total + z_land[index]

    pieces_ref[core, x, 0] = total
    near = sorted(range(1, y_size), key=lambda step: min(step, y_size - step))
    sent = []

    def copy_of(src, dst, sems, index, target):
        return pltpu.make_async_remote_copy(
            src_ref=pieces_ref.at[src], dst_ref=pieces_ref.at[dst],
            send_sem=sems[0].at[index], recv_sem=sems[1].at[index],
            device_id=target, device_id_type=MESH,
        )

    def send(*args):
        copy = copy_of(*args)
        copy.start()
        sent.append(copy)

    y_sems, x_sems, pair_sems = (yg_send, yg_recv), (xg_send, xg_recv), (final_send, final_recv)
    partner = {"af": fiber_at(0, 1)}
    other = (core + 1) % 2
    for place in range(y_size - 1, 0, -1):
        target = {"gz": (y + near[place - 1]) % y_size}
        send((core, x, 0), (core, x, place), y_sems, place - 1, target)
    groups = [pl.ds(0, y_size // 2), pl.ds(y_size // 2, y_size // 2)]
    x_steps = sorted(range(1, x_size), key=lambda step: min(step, x_size - step))
    for number, group in enumerate(groups):
        for place in range(max(group.start, 1), group.start + group.size):
            target = {"gz": (y + near[place - 1]) % y_size}
            copy_of((core, x, 0), (core, x, place), y_sems, place - 1, target).wait_recv()
        mine = (core, x, group)
        for step in reversed(x_steps):
            send(mine, mine, x_sems, (step - 1) * 2 + number, {"gy": (x + step) % x_size})
        send(mine, mine, pair_sems, number, partner)
    for number, group in enumerate(groups):
        for step in x_steps:
            origin = (x + x_size - step) % x_size
            theirs = (core, origin, group)
            copy_of(theirs, theirs, x_sems, (step - 1) * 2 + number, {"gy": origin}).wait_recv()
            send(theirs, theirs, pair_sems, step * 2 + number, partner)
    for number, group in enumerate(groups):
        for step in range(x_size):
            theirs = (other, (x + x_size - step) % x_size, group)
            copy_of(theirs, theirs, pair_sems, step * 2 + number, partner).wait_recv()
    for copy in sent:
        copy.wait_send()


def arrange_kernel(owner_ref, slab_ref, out_ref, owners, slab, sems):
    fibers, _, block_cols = out_ref.shape
    loads = [
        pltpu.make_async_copy(owner_ref, owners, sems.at[0]),
        pltpu.make_async_copy(slab_ref, slab, sems.at[1]),
    ]
    for load in loads:
        load.start()
    loads[0].wait()
    starts = []
    for target in range(fibers):
        source = jnp.int32(0)
        for block in range(1, fibers):
            source = source + jnp.where(owners[0, 0, block] == target, block, 0)
        starts.append(pl.multiple_of(source * block_cols, block_cols))
    loads[1].wait()
    for target in range(fibers):
        out_ref[target] = slab[:, pl.ds(starts[target], block_cols)]


def arrange(owners, slab):
    fibers = owners.shape[-1]
    rows, width = slab.shape
    return pl.pallas_call(
        arrange_kernel,
        out_shape=jax.ShapeDtypeStruct((fibers, rows, width // fibers), slab.dtype),
        in_specs=[pl.BlockSpec(memory_space=pl.ANY)] * 2,
        out_specs=pl.BlockSpec(memory_space=pltpu.VMEM),
        scratch_shapes=[
            pltpu.SMEM(owners.shape, jnp.int32), pltpu.VMEM(slab.shape, slab.dtype), pltpu.SemaphoreType.DMA((2,)),
        ],
    )(owners, slab)


def exchange(arranged):
    sizes = (lax.axis_size("af"), lax.axis_size("gy"), lax.axis_size("gz"))
    fibers, x_size, y_size = sizes
    z_size = fibers // 2
    rows, block_cols = arranged.shape[1:]
    all_rows = rows * fibers
    half = 5 * TILE
    x_rows = half // x_size
    y_rows = max(
        (((p + 1) * (x_rows // 8)) // y_size - (p * (x_rows // 8)) // y_size) for p in range(y_size)
    ) * 8
    dma = pltpu.SemaphoreType.DMA
    f32, bf16 = jnp.float32, jnp.bfloat16
    return pl.pallas_call(
        functools.partial(exchange_kernel, sizes),
        out_shape=(
            jax.ShapeDtypeStruct((all_rows, block_cols), bf16),
            jax.ShapeDtypeStruct((2, x_size, y_size, y_rows, TILE), f32),
        ),
        in_specs=[pl.BlockSpec(memory_space=pltpu.VMEM)],
        out_specs=[pl.BlockSpec(memory_space=pltpu.VMEM)] * 2,
        scratch_shapes=[
            pltpu.VMEM((2 * half, TILE), f32),
            pltpu.VMEM((half, TILE), f32),
            pltpu.VMEM((half, TILE), f32),
            pltpu.VMEM((x_size - 1, x_rows, TILE), f32),
            pltpu.VMEM((x_rows, TILE), f32),
            pltpu.VMEM((y_size - 1, y_rows, TILE), f32),
            pltpu.VMEM((z_size, y_rows, TILE), f32),
            dma((fibers - 1,)), dma((fibers - 1,)), dma, dma,
            dma((x_size - 1,)), dma((x_size - 1,)), dma((y_size - 1,)), dma((y_size - 1,)),
            dma((z_size - 1,)), dma((z_size - 1,)),
            dma((y_size - 1,)), dma((y_size - 1,)),
            dma(((x_size - 1) * 2,)), dma(((x_size - 1) * 2,)),
            dma((x_size * 2,)), dma((x_size * 2,)),
        ],
        compiler_params=pltpu.CompilerParams(collective_id=0, has_side_effects=True, vmem_limit_bytes=32 << 20),
    )(arranged)


NN, NT, TN = ((1,), (0,)), ((1,), (1,)), ((0,), (0,))


def parts_of(a):
    f32, bf16 = jnp.float32, jnp.bfloat16
    high = a.astype(bf16).astype(f32)
    rest = a - high
    middle = rest.astype(bf16).astype(f32)
    return high, middle, rest - middle


def stacked(a, order, axis):
    parts = parts_of(a)
    return jnp.concatenate([parts[k] for k in order], axis=axis).astype(jnp.bfloat16)


LEFT, RIGHT = (0, 0, 1, 1, 0, 2), (0, 1, 0, 1, 2, 0)
MID = 3


def dot_exact(a, b, dims, terms=6):
    (da,), (db,) = dims
    return lax.dot_general(
        stacked(a, LEFT[:terms], da), stacked(b, RIGHT[:terms], db), (dims, ((), ())), preferred_element_type=jnp.float32
    )


def eliminate_strip(strip, final, scales, first):
    f32 = jnp.float32
    shape = (STRIP, TILE)
    lane = lax.broadcasted_iota(jnp.int32, shape, 1)
    sub = lax.broadcasted_iota(jnp.int32, shape, 0)
    heads = [
        jnp.take_along_axis(strip, jnp.full(shape, first + t, jnp.int32), axis=1) for t in range(STRIP)
    ]
    full = strip
    down = strip
    scale = jnp.zeros(shape, f32)
    for t in range(STRIP):
        head = heads[t]
        pivot = jnp.broadcast_to(head[t : t + 1, :], shape)
        inverse = 1.0 / pivot
        scale = jnp.where(sub == t, lax.rsqrt(pivot), scale)
        factor = head * inverse
        here = lane == first + t
        row = jnp.where(here, 1.0, jnp.broadcast_to(full[t : t + 1, :], shape))
        full = jnp.where(sub == t, row * inverse, jnp.where(here, 0.0, full) - factor * row)
        drow = jnp.where(here, 1.0, jnp.broadcast_to(down[t : t + 1, :], shape))
        down = jnp.where(sub > t, jnp.where(here, 0.0, down) - factor * drow, down)
        for u in range(t + 1, STRIP):
            line = jnp.broadcast_to(heads[u][t : t + 1, :], shape)
            heads[u] = jnp.where(sub == t, line * inverse, heads[u] - factor * line)
    final[pl.ds(first, STRIP), :] = down * scale
    scales[pl.ds(first, STRIP), :] = scale
    return full


def stacked_wide(a, order):
    parts = parts_of(a)
    return jnp.concatenate([parts[k] for k in order], axis=0)


def advance(strip, full, work, left, right, first):
    shape = (STRIP, TILE)
    lane = lax.broadcasted_iota(jnp.int32, shape, 1)
    later = jnp.where(lane >= first + STRIP, strip, 0.0)
    left[...] = stacked_wide(later, LEFT).astype(jnp.bfloat16).T
    right[...] = stacked_wide(full, RIGHT).astype(jnp.bfloat16)
    onward = pl.ds(pl.multiple_of(jnp.minimum(first + STRIP, TILE - STRIP), STRIP), STRIP)
    own = (lane >= first) & (lane < first + STRIP)
    following = jnp.where(own, 0.0, work[onward, :])
    sub = lax.broadcasted_iota(jnp.int32, shape, 0)
    change = jnp.zeros(shape, jnp.float32)
    for s in range(STRIP):
        spot = jnp.full(shape, jnp.minimum(first + STRIP + s, TILE - 1), jnp.int32)
        line = jnp.sum(jnp.take_along_axis(strip, spot, axis=1) * full, axis=0, keepdims=True)
        change = jnp.where(sub == s, jnp.broadcast_to(line, shape), change)
    return following - change


def apply_update(work, left, right, first):
    lane = lax.broadcasted_iota(jnp.int32, (TILE, TILE), 1)
    before = (lane >= first - STRIP) & (lane < first)
    update = jnp.dot(left[...], right[...], preferred_element_type=jnp.float32)
    work[...] = jnp.where(before, 0.0, work[...]) - update


def factor_both(works, finals, scales, lefts, rights):
    for left, right in zip(lefts, rights):
        left[...] = jnp.zeros_like(left)
        right[...] = jnp.zeros_like(right)

    def step(index, strips):
        first = pl.multiple_of(index * STRIP, STRIP)
        for work, left, right in zip(works, lefts, rights):
            apply_update(work, left, right, first)
        fulls = [eliminate_strip(v, f, s, first) for v, f, s in zip(strips, finals, scales)]
        return tuple(
            advance(*group, first) for group in zip(strips, fulls, works, lefts, rights)
        )

    lax.fori_loop(0, TILE // STRIP, step, tuple(work[:STRIP, :] for work in works))


def inverse_of(final, scales):
    lane = lax.broadcasted_iota(jnp.int32, (TILE, TILE), 1)
    sub = lax.broadcasted_iota(jnp.int32, (TILE, TILE), 0)
    return jnp.where(lane < sub, final[...], jnp.where(lane == sub, scales[...], 0.0))


def upper_of(final):
    lane = lax.broadcasted_iota(jnp.int32, (TILE, TILE), 1)
    sub = lax.broadcasted_iota(jnp.int32, (TILE, TILE), 0)
    return jnp.where(lane >= sub, final[...], 0.0)


def factor_kernel(
    pieces_ref, start_ref, columns_ref, triangle_ref, basis_ref, core_ref,
    packed_ref, gram, trail, product, work_a, work_b, final_a, final_b, scale_a, scale_b,
    left_a, left_b, right_a, right_b,
):
    count = 4
    cores, x_size, y_size, _, _ = pieces_ref.shape
    tiles = packed_ref.shape[0] // 8 // cores // x_size
    here = lax.axis_index("gz")
    for y in range(y_size):
        step = (here + y_size - y) % y_size
        near = jnp.minimum(step, y_size - step)
        place = 2 * near - jnp.where((step > 0) & (step <= y_size // 2), 1, 0)
        for c in range(cores):
            for x in range(x_size):
                first, last = tiles * y // y_size, tiles * (y + 1) // y_size
                spread = pl.ds(((c * x_size + x) * tiles + first) * 8, (last - first) * 8)
                packed_ref[spread, :] = pieces_ref[c, x, place, : (last - first) * 8, :]
    spot = lambda i, j: pl.ds((i * (i + 1) // 2 + j) * TILE, TILE)
    at = lambda i: pl.ds(i * TILE, TILE)
    for i in range(count):
        for j in range(i + 1):
            block = packed_ref[spot(i, j), :]
            gram[at(i), at(j)] = block
            trail[at(i), at(j)] = block
            if i != j:
                gram[at(j), at(i)] = block.T
                triangle_ref[at(j), at(i)] = jnp.zeros((TILE, TILE), jnp.float32)
    start = start_ref[...]
    image = dot_exact(gram[...], start, NN, MID)
    product[...] = image
    work_b[...] = dot_exact(start, image, TN, MID)
    for k in range(count):
        work_a[...] = trail[at(k), at(k)]
        factor_both(
            (work_a, work_b), (final_a, final_b), (scale_a, scale_b),
            (left_a, left_b), (right_a, right_b),
        )
        turn = inverse_of(final_b, scale_b)
        image = dot_exact(product[...], turn, NT, 6 if k == count - 1 else MID)
        if k == 0 or k == 2:
            product[...] = image
            work_b[...] = dot_exact(image, image, TN, 6 if k == 2 else MID)
        elif k == 1:
            moved = dot_exact(gram[...], image, NN, MID)
            product[...] = moved
            work_b[...] = dot_exact(image, moved, TN, MID)
        else:
            basis_ref[...] = image
            core_ref[...] = lax.dot_general(
                image.astype(jnp.bfloat16), columns_ref[...], (TN, ((), ())), preferred_element_type=jnp.float32
            ).astype(jnp.bfloat16)
        triangle_ref[at(k), at(k)] = upper_of(final_a).T
        if k + 1 < count:
            rest = pl.ds((k + 1) * TILE, (count - 1 - k) * TILE)
            lower = dot_exact(trail[rest, at(k)], inverse_of(final_a, scale_a), NT, 4)
            triangle_ref[rest, at(k)] = lower
            for j in range(k + 1, count):
                tail = pl.ds(j * TILE, (count - j) * TILE)
                skip = (j - k - 1) * TILE
                trail[tail, at(j)] = trail[tail, at(j)] - dot_exact(lower[skip:], lower[skip : skip + TILE], NT, 4)


def factor(pieces, start, columns):
    f32 = jnp.float32
    rows, rank = start.shape
    square = pltpu.VMEM((TILE, TILE), f32)
    wide, tall = pltpu.VMEM((TILE, 6 * STRIP), jnp.bfloat16), pltpu.VMEM((6 * STRIP, TILE), jnp.bfloat16)
    return pl.pallas_call(
        factor_kernel,
        out_shape=(
            jax.ShapeDtypeStruct((rows, rows), f32),
            jax.ShapeDtypeStruct((rows, rank), f32),
            jax.ShapeDtypeStruct((rank, columns.shape[1]), jnp.bfloat16),
        ),
        in_specs=[pl.BlockSpec(memory_space=pltpu.VMEM)] * 3,
        out_specs=[pl.BlockSpec(memory_space=pltpu.VMEM)] * 3,
        scratch_shapes=[
            pltpu.VMEM((10 * TILE, TILE), f32), pltpu.VMEM((rows, rows), f32), pltpu.VMEM((rows, rows), f32), pltpu.VMEM((rows, rank), f32),
            square, square, square, square, square, square,
            wide, wide, tall, tall,
        ],
        compiler_params=pltpu.CompilerParams(vmem_limit_bytes=32 << 20),
    )(pieces, start, columns)


def on_device(slab, block_owner, basis_init):
    columns, packed = exchange(arrange(block_owner, slab))
    return factor(packed, basis_init, columns)


def solution(mesh):
    placed = (P("af", ("gy", "gz")), P("gy", "gz", None), P())
    return jax.shard_map(
        on_device,
        mesh=mesh,
        in_specs=placed,
        out_specs=(P(), P(), P(None, ("gy", "gz", "af"))),
        check_vma=False,
    )
```

```python
import functools
import jax
import jax.numpy as jnp
from jax import lax
from jax.experimental import pallas as pl
from jax.experimental.pallas import tpu as pltpu
from jax.sharding import PartitionSpec as P

TILE = 128
STRIP = 8
exact_mode = lax.Precision.HIGHEST
MESH = pl.DeviceIdType.MESH


def ring_offsets(size):
    return sorted(range(1, size), key=lambda step: -min(step, size - step))


def exchange_kernel(
    sizes, outgoing, columns_ref, pieces_ref,
    part, pair_land, pair_sum, x_land, x_sum, y_land, z_land,
    a2a_send, a2a_recv, pair_send, pair_recv, x_send, x_recv, y_send, y_recv, z_send, z_recv,
    yg_send, yg_recv, xg_send, xg_recv, final_send, final_recv,
):
    fibers, x_size, y_size = sizes
    z_size = fibers // 2
    rows, block_cols = outgoing.shape[1:]
    fiber = lax.axis_index("af")
    x = lax.axis_index("gy")
    y = lax.axis_index("gz")
    z, core = fiber // 2, fiber % 2
    half = pair_sum.shape[0]
    x_rows = x_sum.shape[0]
    y_rows = y_land.shape[1]

    def fiber_at(z_step, core_step):
        return ((z + z_step) % z_size) * 2 + (core + core_step) % 2

    fiber_steps = [(0, 1)] + [(s, c) for s in reversed(ring_offsets(z_size)) for c in (0, 1)]
    barrier = pltpu.get_barrier_semaphore()
    for z_step, core_step in fiber_steps:
        pl.semaphore_signal(barrier, inc=1, device_id={"af": fiber_at(z_step, core_step)}, device_id_type=MESH)
    for step in range(1, y_size):
        pl.semaphore_signal(barrier, inc=1, device_id={"gz": (y + step) % y_size}, device_id_type=MESH)
    for step in range(1, x_size):
        pl.semaphore_signal(barrier, inc=1, device_id={"gy": (x + step) % x_size}, device_id_type=MESH)

    pl.semaphore_wait(barrier, len(fiber_steps) + x_size + y_size - 2)

    my_rows = pl.ds(pl.multiple_of(fiber * rows, rows), rows)
    copies = []
    for index, (z_step, core_step) in enumerate(fiber_steps):
        peer = fiber_at(z_step, core_step)
        copy = pltpu.make_async_remote_copy(
            src_ref=outgoing.at[peer], dst_ref=columns_ref.at[my_rows],
            send_sem=a2a_send.at[index], recv_sem=a2a_recv.at[index],
            device_id={"af": peer}, device_id_type=MESH,
        )
        copy.start()
        copies.append(copy)
    columns_ref[my_rows, :] = outgoing[fiber]
    for copy in copies:
        copy.wait()

    scale = 1.0 / (block_cols * fibers * x_size * y_size)
    pairs = [(i, j) for i in range(4) for j in range(i + 1)]
    per_core = len(pairs) // 2

    def gram_blocks(owner):
        for index in range(per_core):
            (i0, j0), (i1, j1) = pairs[index], pairs[per_core + index]
            i = i0 + owner * (i1 - i0)
            j = j0 + owner * (j1 - j0)
            left = columns_ref[pl.ds(pl.multiple_of(i * TILE, TILE), TILE), :]
            right = columns_ref[pl.ds(pl.multiple_of(j * TILE, TILE), TILE), :]
            product = lax.dot_general(left, right, (((1,), (1,)), ((), ())), preferred_element_type=jnp.float32)
            at = pl.multiple_of(owner * half + index * TILE, TILE)
            part[pl.ds(at, TILE), :] = product * scale

    other = (core + 1) % 2
    gram_blocks(other)
    pair = pltpu.make_async_remote_copy(
        src_ref=part.at[pl.ds(pl.multiple_of(other * half, half), half)], dst_ref=pair_land,
        send_sem=pair_send, recv_sem=pair_recv,
        device_id={"af": fiber_at(0, 1)}, device_id_type=MESH,
    )
    pair.start()
    gram_blocks(core)
    pair.wait()
    my_half = pl.ds(pl.multiple_of(core * half, half), half)
    pair_sum[...] = part[my_half, :] + pair_land[...]

    copies = []
    for step in ring_offsets(x_size):
        peer = (x + step) % x_size
        copy = pltpu.make_async_remote_copy(
            src_ref=pair_sum.at[pl.ds(pl.multiple_of(peer * x_rows, x_rows), x_rows)], dst_ref=x_land.at[step - 1],
            send_sem=x_send.at[step - 1], recv_sem=x_recv.at[step - 1],
            device_id={"gy": peer}, device_id_type=MESH,
        )
        copy.start()
        copies.append(copy)
    for copy in copies:
        copy.wait()
    total = pair_sum[pl.ds(pl.multiple_of(x * x_rows, x_rows), x_rows), :]
    for step in range(1, x_size):
        total = total + x_land[step - 1]
    x_sum[...] = total

    def tile_start(owner):
        return (owner * (x_rows // 8) // y_size) * 8

    copies = []
    for step in ring_offsets(y_size):
        peer = (y + step) % y_size
        copy = pltpu.make_async_remote_copy(
            src_ref=x_sum.at[pl.ds(pl.multiple_of(tile_start(peer), 8), y_rows)], dst_ref=y_land.at[step - 1],
            send_sem=y_send.at[step - 1], recv_sem=y_recv.at[step - 1],
            device_id={"gz": peer}, device_id_type=MESH,
        )
        copy.start()
        copies.append(copy)
    for copy in copies:
        copy.wait()
    total = x_sum[pl.ds(pl.multiple_of(tile_start(y), 8), y_rows), :]
    for step in range(1, y_size):
        total = total + y_land[step - 1]

    z_land[z] = total
    copies = []
    for step in ring_offsets(z_size):
        peer = fiber_at(step, 0)
        copy = pltpu.make_async_remote_copy(
            src_ref=z_land.at[z], dst_ref=z_land.at[z],
            send_sem=z_send.at[step - 1], recv_sem=z_recv.at[step - 1],
            device_id={"af": peer}, device_id_type=MESH,
        )
        copy.start()
        copies.append(copy)
    for copy in copies:
        copy.wait()
    total = z_land[0]
    for index in range(1, z_size):
        total = total + z_land[index]

    pieces_ref[core, x, 0] = total
    near = sorted(range(1, y_size), key=lambda step: min(step, y_size - step))
    sent = []

    def copy_of(src, dst, sems, index, target):
        return pltpu.make_async_remote_copy(
            src_ref=pieces_ref.at[src], dst_ref=pieces_ref.at[dst],
            send_sem=sems[0].at[index], recv_sem=sems[1].at[index],
            device_id=target, device_id_type=MESH,
        )

    def send(*args):
        copy = copy_of(*args)
        copy.start()
        sent.append(copy)

    y_sems, x_sems, pair_sems = (yg_send, yg_recv), (xg_send, xg_recv), (final_send, final_recv)
    partner = {"af": fiber_at(0, 1)}
    other = (core + 1) % 2
    for place in range(y_size - 1, 0, -1):
        target = {"gz": (y + near[place - 1]) % y_size}
        send((core, x, 0), (core, x, place), y_sems, place - 1, target)
    groups = [pl.ds(0, y_size // 2), pl.ds(y_size // 2, y_size // 2)]
    x_steps = sorted(range(1, x_size), key=lambda step: min(step, x_size - step))
    for number, group in enumerate(groups):
        for place in range(max(group.start, 1), group.start + group.size):
            target = {"gz": (y + near[place - 1]) % y_size}
            copy_of((core, x, 0), (core, x, place), y_sems, place - 1, target).wait_recv()
        mine = (core, x, group)
        for step in reversed(x_steps):
            send(mine, mine, x_sems, (step - 1) * 2 + number, {"gy": (x + step) % x_size})
        send(mine, mine, pair_sems, number, partner)
    for number, group in enumerate(groups):
        for step in x_steps:
            origin = (x + x_size - step) % x_size
            theirs = (core, origin, group)
            copy_of(theirs, theirs, x_sems, (step - 1) * 2 + number, {"gy": origin}).wait_recv()
            send(theirs, theirs, pair_sems, step * 2 + number, partner)
    for number, group in enumerate(groups):
        for step in range(x_size):
            theirs = (other, (x + x_size - step) % x_size, group)
            copy_of(theirs, theirs, pair_sems, step * 2 + number, partner).wait_recv()
    for copy in sent:
        copy.wait_send()


def arrange_kernel(owner_ref, slab_ref, out_ref, owners, slab, sems):
    fibers, _, block_cols = out_ref.shape
    loads = [
        pltpu.make_async_copy(owner_ref, owners, sems.at[0]),
        pltpu.make_async_copy(slab_ref, slab, sems.at[1]),
    ]
    for load in loads:
        load.start()
    loads[0].wait()
    starts = []
    for target in range(fibers):
        source = jnp.int32(0)
        for block in range(1, fibers):
            source = source + jnp.where(owners[0, 0, block] == target, block, 0)
        starts.append(pl.multiple_of(source * block_cols, block_cols))
    loads[1].wait()
    for target in range(fibers):
        out_ref[target] = slab[:, pl.ds(starts[target], block_cols)]


def arrange(owners, slab):
    fibers = owners.shape[-1]
    rows, width = slab.shape
    return pl.pallas_call(
        arrange_kernel,
        out_shape=jax.ShapeDtypeStruct((fibers, rows, width // fibers), slab.dtype),
        in_specs=[pl.BlockSpec(memory_space=pl.ANY)] * 2,
        out_specs=pl.BlockSpec(memory_space=pltpu.VMEM),
        scratch_shapes=[
            pltpu.SMEM(owners.shape, jnp.int32), pltpu.VMEM(slab.shape, slab.dtype), pltpu.SemaphoreType.DMA((2,)),
        ],
    )(owners, slab)


def exchange(arranged):
    sizes = (lax.axis_size("af"), lax.axis_size("gy"), lax.axis_size("gz"))
    fibers, x_size, y_size = sizes
    z_size = fibers // 2
    rows, block_cols = arranged.shape[1:]
    all_rows = rows * fibers
    half = 5 * TILE
    x_rows = half // x_size
    y_rows = max(
        (((p + 1) * (x_rows // 8)) // y_size - (p * (x_rows // 8)) // y_size) for p in range(y_size)
    ) * 8
    dma = pltpu.SemaphoreType.DMA
    f32, bf16 = jnp.float32, jnp.bfloat16
    return pl.pallas_call(
        functools.partial(exchange_kernel, sizes),
        out_shape=(
            jax.ShapeDtypeStruct((all_rows, block_cols), bf16),
            jax.ShapeDtypeStruct((2, x_size, y_size, y_rows, TILE), f32),
        ),
        in_specs=[pl.BlockSpec(memory_space=pltpu.VMEM)],
        out_specs=[pl.BlockSpec(memory_space=pltpu.VMEM)] * 2,
        scratch_shapes=[
            pltpu.VMEM((2 * half, TILE), f32),
            pltpu.VMEM((half, TILE), f32),
            pltpu.VMEM((half, TILE), f32),
            pltpu.VMEM((x_size - 1, x_rows, TILE), f32),
            pltpu.VMEM((x_rows, TILE), f32),
            pltpu.VMEM((y_size - 1, y_rows, TILE), f32),
            pltpu.VMEM((z_size, y_rows, TILE), f32),
            dma((fibers - 1,)), dma((fibers - 1,)), dma, dma,
            dma((x_size - 1,)), dma((x_size - 1,)), dma((y_size - 1,)), dma((y_size - 1,)),
            dma((z_size - 1,)), dma((z_size - 1,)),
            dma((y_size - 1,)), dma((y_size - 1,)),
            dma(((x_size - 1) * 2,)), dma(((x_size - 1) * 2,)),
            dma((x_size * 2,)), dma((x_size * 2,)),
        ],
        compiler_params=pltpu.CompilerParams(collective_id=0, has_side_effects=True, vmem_limit_bytes=32 << 20),
    )(arranged)


NN, NT, TN = ((1,), (0,)), ((1,), (1,)), ((0,), (0,))


def parts_of(a):
    f32, bf16 = jnp.float32, jnp.bfloat16
    high = a.astype(bf16).astype(f32)
    rest = a - high
    middle = rest.astype(bf16).astype(f32)
    return high, middle, rest - middle


def stacked(a, order, axis):
    parts = parts_of(a)
    return jnp.concatenate([parts[k] for k in order], axis=axis).astype(jnp.bfloat16)


LEFT, RIGHT = (0, 0, 1, 1, 0, 2), (0, 1, 0, 1, 2, 0)
MID = 3


def dot_exact(a, b, dims, terms=6):
    (da,), (db,) = dims
    return lax.dot_general(
        stacked(a, LEFT[:terms], da), stacked(b, RIGHT[:terms], db), (dims, ((), ())), preferred_element_type=jnp.float32
    )


def eliminate_strip(strip, final, scales, first):
    f32 = jnp.float32
    shape = (STRIP, TILE)
    lane = lax.broadcasted_iota(jnp.int32, shape, 1)
    sub = lax.broadcasted_iota(jnp.int32, shape, 0)
    heads = [
        jnp.take_along_axis(strip, jnp.full(shape, first + t, jnp.int32), axis=1) for t in range(STRIP)
    ]
    full = strip
    down = strip
    scale = jnp.zeros(shape, f32)
    for t in range(STRIP):
        head = heads[t]
        pivot = jnp.broadcast_to(head[t : t + 1, :], shape)
        inverse = 1.0 / pivot
        scale = jnp.where(sub == t, lax.rsqrt(pivot), scale)
        factor = head * inverse
        here = lane == first + t
        row = jnp.where(here, 1.0, jnp.broadcast_to(full[t : t + 1, :], shape))
        full = jnp.where(sub == t, row * inverse, jnp.where(here, 0.0, full) - factor * row)
        drow = jnp.where(here, 1.0, jnp.broadcast_to(down[t : t + 1, :], shape))
        down = jnp.where(sub > t, jnp.where(here, 0.0, down) - factor * drow, down)
        for u in range(t + 1, STRIP):
            line = jnp.broadcast_to(heads[u][t : t + 1, :], shape)
            heads[u] = jnp.where(sub == t, line * inverse, heads[u] - factor * line)
    final[pl.ds(first, STRIP), :] = down * scale
    scales[pl.ds(first, STRIP), :] = scale
    return full


def stacked_wide(a, order):
    parts = parts_of(a)
    return jnp.concatenate([parts[k] for k in order], axis=0)


def advance(strip, full, work, left, right, first):
    shape = (STRIP, TILE)
    lane = lax.broadcasted_iota(jnp.int32, shape, 1)
    later = jnp.where(lane >= first + STRIP, strip, 0.0)
    left[...] = stacked_wide(later, LEFT).astype(jnp.bfloat16).T
    right[...] = stacked_wide(full, RIGHT).astype(jnp.bfloat16)
    onward = pl.ds(pl.multiple_of(jnp.minimum(first + STRIP, TILE - STRIP), STRIP), STRIP)
    own = (lane >= first) & (lane < first + STRIP)
    following = jnp.where(own, 0.0, work[onward, :])
    sub = lax.broadcasted_iota(jnp.int32, shape, 0)
    change = jnp.zeros(shape, jnp.float32)
    for s in range(STRIP):
        spot = jnp.full(shape, jnp.minimum(first + STRIP + s, TILE - 1), jnp.int32)
        line = jnp.sum(jnp.take_along_axis(strip, spot, axis=1) * full, axis=0, keepdims=True)
        change = jnp.where(sub == s, jnp.broadcast_to(line, shape), change)
    return following - change


def apply_update(work, left, right, first):
    lane = lax.broadcasted_iota(jnp.int32, (TILE, TILE), 1)
    before = (lane >= first - STRIP) & (lane < first)
    update = jnp.dot(left[...], right[...], preferred_element_type=jnp.float32)
    work[...] = jnp.where(before, 0.0, work[...]) - update


def factor_both(works, finals, scales, lefts, rights):
    for left, right in zip(lefts, rights):
        left[...] = jnp.zeros_like(left)
        right[...] = jnp.zeros_like(right)

    def step(index, strips):
        first = pl.multiple_of(index * STRIP, STRIP)
        for work, left, right in zip(works, lefts, rights):
            apply_update(work, left, right, first)
        fulls = [eliminate_strip(v, f, s, first) for v, f, s in zip(strips, finals, scales)]
        return tuple(
            advance(*group, first) for group in zip(strips, fulls, works, lefts, rights)
        )

    lax.fori_loop(0, TILE // STRIP, step, tuple(work[:STRIP, :] for work in works), unroll=4)


def inverse_of(final, scales):
    lane = lax.broadcasted_iota(jnp.int32, (TILE, TILE), 1)
    sub = lax.broadcasted_iota(jnp.int32, (TILE, TILE), 0)
    return jnp.where(lane < sub, final[...], jnp.where(lane == sub, scales[...], 0.0))


def upper_of(final):
    lane = lax.broadcasted_iota(jnp.int32, (TILE, TILE), 1)
    sub = lax.broadcasted_iota(jnp.int32, (TILE, TILE), 0)
    return jnp.where(lane >= sub, final[...], 0.0)


def factor_kernel(
    pieces_ref, start_ref, columns_ref, triangle_ref, basis_ref, core_ref,
    packed_ref, gram, trail, product, work_a, work_b, final_a, final_b, scale_a, scale_b,
    left_a, left_b, right_a, right_b,
):
    count = 4
    cores, x_size, y_size, _, _ = pieces_ref.shape
    tiles = packed_ref.shape[0] // 8 // cores // x_size
    here = lax.axis_index("gz")
    for y in range(y_size):
        step = (here + y_size - y) % y_size
        near = jnp.minimum(step, y_size - step)
        place = 2 * near - jnp.where((step > 0) & (step <= y_size // 2), 1, 0)
        for c in range(cores):
            for x in range(x_size):
                first, last = tiles * y // y_size, tiles * (y + 1) // y_size
                spread = pl.ds(((c * x_size + x) * tiles + first) * 8, (last - first) * 8)
                packed_ref[spread, :] = pieces_ref[c, x, place, : (last - first) * 8, :]
    spot = lambda i, j: pl.ds((i * (i + 1) // 2 + j) * TILE, TILE)
    at = lambda i: pl.ds(i * TILE, TILE)
    for i in range(count):
        for j in range(i + 1):
            block = packed_ref[spot(i, j), :]
            gram[at(i), at(j)] = block
            trail[at(i), at(j)] = block
            if i != j:
                gram[at(j), at(i)] = block.T
                triangle_ref[at(j), at(i)] = jnp.zeros((TILE, TILE), jnp.float32)
    start = start_ref[...]
    image = dot_exact(gram[...], start, NN, MID)
    product[...] = image
    work_b[...] = dot_exact(start, image, TN, MID)
    for k in range(count):
        work_a[...] = trail[at(k), at(k)]
        factor_both(
            (work_a, work_b), (final_a, final_b), (scale_a, scale_b),
            (left_a, left_b), (right_a, right_b),
        )
        turn = inverse_of(final_b, scale_b)
        image = dot_exact(product[...], turn, NT, 6 if k == count - 1 else MID)
        if k == 0 or k == 2:
            product[...] = image
            work_b[...] = dot_exact(image, image, TN, 6 if k == 2 else MID)
        elif k == 1:
            moved = dot_exact(gram[...], image, NN, MID)
            product[...] = moved
            work_b[...] = dot_exact(image, moved, TN, MID)
        else:
            basis_ref[...] = image
            core_ref[...] = lax.dot_general(
                image.astype(jnp.bfloat16), columns_ref[...], (TN, ((), ())), preferred_element_type=jnp.float32
            ).astype(jnp.bfloat16)
        triangle_ref[at(k), at(k)] = upper_of(final_a).T
        if k + 1 < count:
            rest = pl.ds((k + 1) * TILE, (count - 1 - k) * TILE)
            lower = dot_exact(trail[rest, at(k)], inverse_of(final_a, scale_a), NT, 4)
            triangle_ref[rest, at(k)] = lower
            for j in range(k + 1, count):
                tail = pl.ds(j * TILE, (count - j) * TILE)
                skip = (j - k - 1) * TILE
                trail[tail, at(j)] = trail[tail, at(j)] - dot_exact(lower[skip:], lower[skip : skip + TILE], NT, 4)


def factor(pieces, start, columns):
    f32 = jnp.float32
    rows, rank = start.shape
    square = pltpu.VMEM((TILE, TILE), f32)
    wide, tall = pltpu.VMEM((TILE, 6 * STRIP), jnp.bfloat16), pltpu.VMEM((6 * STRIP, TILE), jnp.bfloat16)
    return pl.pallas_call(
        factor_kernel,
        out_shape=(
            jax.ShapeDtypeStruct((rows, rows), f32),
            jax.ShapeDtypeStruct((rows, rank), f32),
            jax.ShapeDtypeStruct((rank, columns.shape[1]), jnp.bfloat16),
        ),
        in_specs=[pl.BlockSpec(memory_space=pltpu.VMEM)] * 3,
        out_specs=[pl.BlockSpec(memory_space=pltpu.VMEM)] * 3,
        scratch_shapes=[
            pltpu.VMEM((10 * TILE, TILE), f32), pltpu.VMEM((rows, rows), f32), pltpu.VMEM((rows, rows), f32), pltpu.VMEM((rows, rank), f32),
            square, square, square, square, square, square,
            wide, wide, tall, tall,
        ],
        compiler_params=pltpu.CompilerParams(vmem_limit_bytes=32 << 20),
    )(pieces, start, columns)


def on_device(slab, block_owner, basis_init):
    columns, packed = exchange(arrange(block_owner, slab))
    return factor(packed, basis_init, columns)


def solution(mesh):
    placed = (P("af", ("gy", "gz")), P("gy", "gz", None), P())
    return jax.shard_map(
        on_device,
        mesh=mesh,
        in_specs=placed,
        out_specs=(P(), P(), P(None, ("gy", "gz", "af"))),
        check_vma=False,
    )
```

```python
import functools
import jax
import jax.numpy as jnp
from jax import lax
from jax.experimental import pallas as pl
from jax.experimental.pallas import tpu as pltpu
from jax.sharding import PartitionSpec as P

TILE = 128
STRIP = 8
exact_mode = lax.Precision.HIGHEST
MESH = pl.DeviceIdType.MESH


def ring_offsets(size):
    return sorted(range(1, size), key=lambda step: -min(step, size - step))


def exchange_kernel(
    sizes, outgoing, columns_ref, pieces_ref,
    part, pair_land, pair_sum, x_land, x_sum, y_land, z_land,
    a2a_send, a2a_recv, pair_send, pair_recv, x_send, x_recv, y_send, y_recv, z_send, z_recv,
    yg_send, yg_recv, xg_send, xg_recv, final_send, final_recv,
):
    fibers, x_size, y_size = sizes
    z_size = fibers // 2
    rows, block_cols = outgoing.shape[1:]
    fiber = lax.axis_index("af")
    x = lax.axis_index("gy")
    y = lax.axis_index("gz")
    z, core = fiber // 2, fiber % 2
    half = pair_sum.shape[0]
    x_rows = x_sum.shape[0]
    y_rows = y_land.shape[1]

    def fiber_at(z_step, core_step):
        return ((z + z_step) % z_size) * 2 + (core + core_step) % 2

    fiber_steps = [(0, 1)] + [(s, c) for s in reversed(ring_offsets(z_size)) for c in (0, 1)]
    barrier = pltpu.get_barrier_semaphore()
    for z_step, core_step in fiber_steps:
        pl.semaphore_signal(barrier, inc=1, device_id={"af": fiber_at(z_step, core_step)}, device_id_type=MESH)
    for step in range(1, y_size):
        pl.semaphore_signal(barrier, inc=1, device_id={"gz": (y + step) % y_size}, device_id_type=MESH)
    for step in range(1, x_size):
        pl.semaphore_signal(barrier, inc=1, device_id={"gy": (x + step) % x_size}, device_id_type=MESH)

    pl.semaphore_wait(barrier, len(fiber_steps) + x_size + y_size - 2)

    my_rows = pl.ds(pl.multiple_of(fiber * rows, rows), rows)
    copies = []
    for index, (z_step, core_step) in enumerate(fiber_steps):
        peer = fiber_at(z_step, core_step)
        copy = pltpu.make_async_remote_copy(
            src_ref=outgoing.at[peer], dst_ref=columns_ref.at[my_rows],
            send_sem=a2a_send.at[index], recv_sem=a2a_recv.at[index],
            device_id={"af": peer}, device_id_type=MESH,
        )
        copy.start()
        copies.append(copy)
    columns_ref[my_rows, :] = outgoing[fiber]
    for copy in copies:
        copy.wait()

    scale = 1.0 / (block_cols * fibers * x_size * y_size)
    pairs = [(i, j) for i in range(4) for j in range(i + 1)]
    per_core = len(pairs) // 2

    def gram_blocks(owner):
        for index in range(per_core):
            (i0, j0), (i1, j1) = pairs[index], pairs[per_core + index]
            i = i0 + owner * (i1 - i0)
            j = j0 + owner * (j1 - j0)
            left = columns_ref[pl.ds(pl.multiple_of(i * TILE, TILE), TILE), :]
            right = columns_ref[pl.ds(pl.multiple_of(j * TILE, TILE), TILE), :]
            product = lax.dot_general(left, right, (((1,), (1,)), ((), ())), preferred_element_type=jnp.float32)
            at = pl.multiple_of(owner * half + index * TILE, TILE)
            part[pl.ds(at, TILE), :] = product * scale

    other = (core + 1) % 2
    gram_blocks(other)
    pair = pltpu.make_async_remote_copy(
        src_ref=part.at[pl.ds(pl.multiple_of(other * half, half), half)], dst_ref=pair_land,
        send_sem=pair_send, recv_sem=pair_recv,
        device_id={"af": fiber_at(0, 1)}, device_id_type=MESH,
    )
    pair.start()
    gram_blocks(core)
    pair.wait()
    my_half = pl.ds(pl.multiple_of(core * half, half), half)
    pair_sum[...] = part[my_half, :] + pair_land[...]

    copies = []
    for step in ring_offsets(x_size):
        peer = (x + step) % x_size
        copy = pltpu.make_async_remote_copy(
            src_ref=pair_sum.at[pl.ds(pl.multiple_of(peer * x_rows, x_rows), x_rows)], dst_ref=x_land.at[step - 1],
            send_sem=x_send.at[step - 1], recv_sem=x_recv.at[step - 1],
            device_id={"gy": peer}, device_id_type=MESH,
        )
        copy.start()
        copies.append(copy)
    for copy in copies:
        copy.wait()
    total = pair_sum[pl.ds(pl.multiple_of(x * x_rows, x_rows), x_rows), :]
    for step in range(1, x_size):
        total = total + x_land[step - 1]
    x_sum[...] = total

    def tile_start(owner):
        return (owner * (x_rows // 8) // y_size) * 8

    copies = []
    for step in ring_offsets(y_size):
        peer = (y + step) % y_size
        copy = pltpu.make_async_remote_copy(
            src_ref=x_sum.at[pl.ds(pl.multiple_of(tile_start(peer), 8), y_rows)], dst_ref=y_land.at[step - 1],
            send_sem=y_send.at[step - 1], recv_sem=y_recv.at[step - 1],
            device_id={"gz": peer}, device_id_type=MESH,
        )
        copy.start()
        copies.append(copy)
    for copy in copies:
        copy.wait()
    total = x_sum[pl.ds(pl.multiple_of(tile_start(y), 8), y_rows), :]
    for step in range(1, y_size):
        total = total + y_land[step - 1]

    z_land[z] = total
    copies = []
    for step in ring_offsets(z_size):
        peer = fiber_at(step, 0)
        copy = pltpu.make_async_remote_copy(
            src_ref=z_land.at[z], dst_ref=z_land.at[z],
            send_sem=z_send.at[step - 1], recv_sem=z_recv.at[step - 1],
            device_id={"af": peer}, device_id_type=MESH,
        )
        copy.start()
        copies.append(copy)
    for copy in copies:
        copy.wait()
    total = z_land[0]
    for index in range(1, z_size):
        total = total + z_land[index]

    pieces_ref[core, x, 0] = total
    near = sorted(range(1, y_size), key=lambda step: min(step, y_size - step))
    sent = []

    def copy_of(src, dst, sems, index, target):
        return pltpu.make_async_remote_copy(
            src_ref=pieces_ref.at[src], dst_ref=pieces_ref.at[dst],
            send_sem=sems[0].at[index], recv_sem=sems[1].at[index],
            device_id=target, device_id_type=MESH,
        )

    def send(*args):
        copy = copy_of(*args)
        copy.start()
        sent.append(copy)

    y_sems, x_sems, pair_sems = (yg_send, yg_recv), (xg_send, xg_recv), (final_send, final_recv)
    partner = {"af": fiber_at(0, 1)}
    other = (core + 1) % 2
    for place in range(y_size - 1, 0, -1):
        target = {"gz": (y + near[place - 1]) % y_size}
        send((core, x, 0), (core, x, place), y_sems, place - 1, target)
    groups = [pl.ds(0, y_size)]
    x_steps = sorted(range(1, x_size), key=lambda step: min(step, x_size - step))
    for number, group in enumerate(groups):
        for place in range(max(group.start, 1), group.start + group.size):
            target = {"gz": (y + near[place - 1]) % y_size}
            copy_of((core, x, 0), (core, x, place), y_sems, place - 1, target).wait_recv()
        mine = (core, x, group)
        for step in reversed(x_steps):
            send(mine, mine, x_sems, (step - 1) * 2 + number, {"gy": (x + step) % x_size})
        send(mine, mine, pair_sems, number, partner)
    for number, group in enumerate(groups):
        for step in x_steps:
            origin = (x + x_size - step) % x_size
            theirs = (core, origin, group)
            copy_of(theirs, theirs, x_sems, (step - 1) * 2 + number, {"gy": origin}).wait_recv()
            send(theirs, theirs, pair_sems, step * 2 + number, partner)
    for number, group in enumerate(groups):
        for step in range(x_size):
            theirs = (other, (x + x_size - step) % x_size, group)
            copy_of(theirs, theirs, pair_sems, step * 2 + number, partner).wait_recv()
    for copy in sent:
        copy.wait_send()


def arrange_kernel(owner_ref, slab_ref, out_ref, owners, slab, sems):
    fibers, _, block_cols = out_ref.shape
    loads = [
        pltpu.make_async_copy(owner_ref, owners, sems.at[0]),
        pltpu.make_async_copy(slab_ref, slab, sems.at[1]),
    ]
    for load in loads:
        load.start()
    loads[0].wait()
    starts = []
    for target in range(fibers):
        source = jnp.int32(0)
        for block in range(1, fibers):
            source = source + jnp.where(owners[0, 0, block] == target, block, 0)
        starts.append(pl.multiple_of(source * block_cols, block_cols))
    loads[1].wait()
    for target in range(fibers):
        out_ref[target] = slab[:, pl.ds(starts[target], block_cols)]


def arrange(owners, slab):
    fibers = owners.shape[-1]
    rows, width = slab.shape
    return pl.pallas_call(
        arrange_kernel,
        out_shape=jax.ShapeDtypeStruct((fibers, rows, width // fibers), slab.dtype),
        in_specs=[pl.BlockSpec(memory_space=pl.ANY)] * 2,
        out_specs=pl.BlockSpec(memory_space=pltpu.VMEM),
        scratch_shapes=[
            pltpu.SMEM(owners.shape, jnp.int32), pltpu.VMEM(slab.shape, slab.dtype), pltpu.SemaphoreType.DMA((2,)),
        ],
    )(owners, slab)


def exchange(arranged):
    sizes = (lax.axis_size("af"), lax.axis_size("gy"), lax.axis_size("gz"))
    fibers, x_size, y_size = sizes
    z_size = fibers // 2
    rows, block_cols = arranged.shape[1:]
    all_rows = rows * fibers
    half = 5 * TILE
    x_rows = half // x_size
    y_rows = max(
        (((p + 1) * (x_rows // 8)) // y_size - (p * (x_rows // 8)) // y_size) for p in range(y_size)
    ) * 8
    dma = pltpu.SemaphoreType.DMA
    f32, bf16 = jnp.float32, jnp.bfloat16
    return pl.pallas_call(
        functools.partial(exchange_kernel, sizes),
        out_shape=(
            jax.ShapeDtypeStruct((all_rows, block_cols), bf16),
            jax.ShapeDtypeStruct((2, x_size, y_size, y_rows, TILE), f32),
        ),
        in_specs=[pl.BlockSpec(memory_space=pltpu.VMEM)],
        out_specs=[pl.BlockSpec(memory_space=pltpu.VMEM)] * 2,
        scratch_shapes=[
            pltpu.VMEM((2 * half, TILE), f32),
            pltpu.VMEM((half, TILE), f32),
            pltpu.VMEM((half, TILE), f32),
            pltpu.VMEM((x_size - 1, x_rows, TILE), f32),
            pltpu.VMEM((x_rows, TILE), f32),
            pltpu.VMEM((y_size - 1, y_rows, TILE), f32),
            pltpu.VMEM((z_size, y_rows, TILE), f32),
            dma((fibers - 1,)), dma((fibers - 1,)), dma, dma,
            dma((x_size - 1,)), dma((x_size - 1,)), dma((y_size - 1,)), dma((y_size - 1,)),
            dma((z_size - 1,)), dma((z_size - 1,)),
            dma((y_size - 1,)), dma((y_size - 1,)),
            dma(((x_size - 1) * 2,)), dma(((x_size - 1) * 2,)),
            dma((x_size * 2,)), dma((x_size * 2,)),
        ],
        compiler_params=pltpu.CompilerParams(collective_id=0, has_side_effects=True, vmem_limit_bytes=32 << 20),
    )(arranged)


NN, NT, TN = ((1,), (0,)), ((1,), (1,)), ((0,), (0,))


def parts_of(a):
    f32, bf16 = jnp.float32, jnp.bfloat16
    high = a.astype(bf16).astype(f32)
    rest = a - high
    middle = rest.astype(bf16).astype(f32)
    return high, middle, rest - middle


def stacked(a, order, axis):
    parts = parts_of(a)
    return jnp.concatenate([parts[k] for k in order], axis=axis).astype(jnp.bfloat16)


LEFT, RIGHT = (0, 0, 1, 1, 0, 2), (0, 1, 0, 1, 2, 0)
MID = 3


def dot_exact(a, b, dims, terms=6):
    (da,), (db,) = dims
    return lax.dot_general(
        stacked(a, LEFT[:terms], da), stacked(b, RIGHT[:terms], db), (dims, ((), ())), preferred_element_type=jnp.float32
    )


def eliminate_strip(strip, final, scales, first):
    f32 = jnp.float32
    shape = (STRIP, TILE)
    lane = lax.broadcasted_iota(jnp.int32, shape, 1)
    sub = lax.broadcasted_iota(jnp.int32, shape, 0)
    heads = [
        jnp.take_along_axis(strip, jnp.full(shape, first + t, jnp.int32), axis=1) for t in range(STRIP)
    ]
    full = strip
    down = strip
    scale = jnp.zeros(shape, f32)
    for t in range(STRIP):
        head = heads[t]
        pivot = jnp.broadcast_to(head[t : t + 1, :], shape)
        inverse = 1.0 / pivot
        scale = jnp.where(sub == t, lax.rsqrt(pivot), scale)
        factor = head * inverse
        here = lane == first + t
        row = jnp.where(here, 1.0, jnp.broadcast_to(full[t : t + 1, :], shape))
        full = jnp.where(sub == t, row * inverse, jnp.where(here, 0.0, full) - factor * row)
        drow = jnp.where(here, 1.0, jnp.broadcast_to(down[t : t + 1, :], shape))
        down = jnp.where(sub > t, jnp.where(here, 0.0, down) - factor * drow, down)
        for u in range(t + 1, STRIP):
            line = jnp.broadcast_to(heads[u][t : t + 1, :], shape)
            heads[u] = jnp.where(sub == t, line * inverse, heads[u] - factor * line)
    final[pl.ds(first, STRIP), :] = down * scale
    scales[pl.ds(first, STRIP), :] = scale
    return full


def stacked_wide(a, order):
    parts = parts_of(a)
    return jnp.concatenate([parts[k] for k in order], axis=0)


def advance(strip, full, work, left, right, first):
    shape = (STRIP, TILE)
    lane = lax.broadcasted_iota(jnp.int32, shape, 1)
    later = jnp.where(lane >= first + STRIP, strip, 0.0)
    left[...] = stacked_wide(later, LEFT).astype(jnp.bfloat16).T
    right[...] = stacked_wide(full, RIGHT).astype(jnp.bfloat16)
    onward = pl.ds(pl.multiple_of(jnp.minimum(first + STRIP, TILE - STRIP), STRIP), STRIP)
    own = (lane >= first) & (lane < first + STRIP)
    following = jnp.where(own, 0.0, work[onward, :])
    sub = lax.broadcasted_iota(jnp.int32, shape, 0)
    change = jnp.zeros(shape, jnp.float32)
    for s in range(STRIP):
        spot = jnp.full(shape, jnp.minimum(first + STRIP + s, TILE - 1), jnp.int32)
        line = jnp.sum(jnp.take_along_axis(strip, spot, axis=1) * full, axis=0, keepdims=True)
        change = jnp.where(sub == s, jnp.broadcast_to(line, shape), change)
    return following - change


def apply_update(work, left, right, first):
    lane = lax.broadcasted_iota(jnp.int32, (TILE, TILE), 1)
    before = (lane >= first - STRIP) & (lane < first)
    update = jnp.dot(left[...], right[...], preferred_element_type=jnp.float32)
    work[...] = jnp.where(before, 0.0, work[...]) - update


def factor_both(works, finals, scales, lefts, rights):
    for left, right in zip(lefts, rights):
        left[...] = jnp.zeros_like(left)
        right[...] = jnp.zeros_like(right)

    def step(index, strips):
        first = pl.multiple_of(index * STRIP, STRIP)
        for work, left, right in zip(works, lefts, rights):
            apply_update(work, left, right, first)
        fulls = [eliminate_strip(v, f, s, first) for v, f, s in zip(strips, finals, scales)]
        return tuple(
            advance(*group, first) for group in zip(strips, fulls, works, lefts, rights)
        )

    lax.fori_loop(0, TILE // STRIP, step, tuple(work[:STRIP, :] for work in works))


def inverse_of(final, scales):
    lane = lax.broadcasted_iota(jnp.int32, (TILE, TILE), 1)
    sub = lax.broadcasted_iota(jnp.int32, (TILE, TILE), 0)
    return jnp.where(lane < sub, final[...], jnp.where(lane == sub, scales[...], 0.0))


def upper_of(final):
    lane = lax.broadcasted_iota(jnp.int32, (TILE, TILE), 1)
    sub = lax.broadcasted_iota(jnp.int32, (TILE, TILE), 0)
    return jnp.where(lane >= sub, final[...], 0.0)


def factor_kernel(
    pieces_ref, start_ref, columns_ref, triangle_ref, basis_ref, core_ref,
    packed_ref, gram, trail, product, work_a, work_b, final_a, final_b, scale_a, scale_b,
    left_a, left_b, right_a, right_b,
):
    count = 4
    cores, x_size, y_size, _, _ = pieces_ref.shape
    tiles = packed_ref.shape[0] // 8 // cores // x_size
    here = lax.axis_index("gz")
    for y in range(y_size):
        step = (here + y_size - y) % y_size
        near = jnp.minimum(step, y_size - step)
        place = 2 * near - jnp.where((step > 0) & (step <= y_size // 2), 1, 0)
        for c in range(cores):
            for x in range(x_size):
                first, last = tiles * y // y_size, tiles * (y + 1) // y_size
                spread = pl.ds(((c * x_size + x) * tiles + first) * 8, (last - first) * 8)
                packed_ref[spread, :] = pieces_ref[c, x, place, : (last - first) * 8, :]
    spot = lambda i, j: pl.ds((i * (i + 1) // 2 + j) * TILE, TILE)
    at = lambda i: pl.ds(i * TILE, TILE)
    for i in range(count):
        for j in range(i + 1):
            block = packed_ref[spot(i, j), :]
            gram[at(i), at(j)] = block
            trail[at(i), at(j)] = block
            if i != j:
                gram[at(j), at(i)] = block.T
                triangle_ref[at(j), at(i)] = jnp.zeros((TILE, TILE), jnp.float32)
    start = start_ref[...]
    image = dot_exact(gram[...], start, NN, MID)
    product[...] = image
    work_b[...] = dot_exact(start, image, TN, MID)
    for k in range(count):
        work_a[...] = trail[at(k), at(k)]
        factor_both(
            (work_a, work_b), (final_a, final_b), (scale_a, scale_b),
            (left_a, left_b), (right_a, right_b),
        )
        turn = inverse_of(final_b, scale_b)
        image = dot_exact(product[...], turn, NT, 6 if k == count - 1 else MID)
        if k == 0 or k == 2:
            product[...] = image
            work_b[...] = dot_exact(image, image, TN, 6 if k == 2 else MID)
        elif k == 1:
            moved = dot_exact(gram[...], image, NN, MID)
            product[...] = moved
            work_b[...] = dot_exact(image, moved, TN, MID)
        else:
            basis_ref[...] = image
            core_ref[...] = lax.dot_general(
                image.astype(jnp.bfloat16), columns_ref[...], (TN, ((), ())), preferred_element_type=jnp.float32
            ).astype(jnp.bfloat16)
        triangle_ref[at(k), at(k)] = upper_of(final_a).T
        if k + 1 < count:
            rest = pl.ds((k + 1) * TILE, (count - 1 - k) * TILE)
            lower = dot_exact(trail[rest, at(k)], inverse_of(final_a, scale_a), NT, 4)
            triangle_ref[rest, at(k)] = lower
            for j in range(k + 1, count):
                tail = pl.ds(j * TILE, (count - j) * TILE)
                skip = (j - k - 1) * TILE
                trail[tail, at(j)] = trail[tail, at(j)] - dot_exact(lower[skip:], lower[skip : skip + TILE], NT, 4)


def factor(pieces, start, columns):
    f32 = jnp.float32
    rows, rank = start.shape
    square = pltpu.VMEM((TILE, TILE), f32)
    wide, tall = pltpu.VMEM((TILE, 6 * STRIP), jnp.bfloat16), pltpu.VMEM((6 * STRIP, TILE), jnp.bfloat16)
    return pl.pallas_call(
        factor_kernel,
        out_shape=(
            jax.ShapeDtypeStruct((rows, rows), f32),
            jax.ShapeDtypeStruct((rows, rank), f32),
            jax.ShapeDtypeStruct((rank, columns.shape[1]), jnp.bfloat16),
        ),
        in_specs=[pl.BlockSpec(memory_space=pltpu.VMEM)] * 3,
        out_specs=[pl.BlockSpec(memory_space=pltpu.VMEM)] * 3,
        scratch_shapes=[
            pltpu.VMEM((10 * TILE, TILE), f32), pltpu.VMEM((rows, rows), f32), pltpu.VMEM((rows, rows), f32), pltpu.VMEM((rows, rank), f32),
            square, square, square, square, square, square,
            wide, wide, tall, tall,
        ],
        compiler_params=pltpu.CompilerParams(vmem_limit_bytes=32 << 20),
    )(pieces, start, columns)


def on_device(slab, block_owner, basis_init):
    columns, packed = exchange(arrange(block_owner, slab))
    return factor(packed, basis_init, columns)


def solution(mesh):
    placed = (P("af", ("gy", "gz")), P("gy", "gz", None), P())
    return jax.shard_map(
        on_device,
        mesh=mesh,
        in_specs=placed,
        out_specs=(P(), P(), P(None, ("gy", "gz", "af"))),
        check_vma=False,
    )
```
